256 devices in a mesh: scen: 16 (over z, core), clus: 16 (over y, x).
Axes of the slice: x: 4, y: 4, z: 8, core: 2. Of those that a mesh axis runs over, the one named last changes fastest.
Arguments:
- duals: bfloat16 [16384, 2, 128], P(('scen', 'clus')), may hold values from -6 to 6
- blocks: bfloat16 [16384, 2, 128, 128], P(('scen', 'clus')), may hold values from -0.5 to 0.5
- prob: float32 [16384], P(('scen', 'clus')), may hold values from 0.25 to 4
- cluster_map: int32 [16384], P(('scen', 'clus')), may hold values from 0 to 15
- block_cols: int32 [16384, 2], P(('scen', 'clus')), may hold values from 0 to 255
- counts: int32 [256], P(('scen', 'clus')), may hold values from 16 to 64, as said below
- cut_owner_rows: int32 [256], replicated, may hold values from 0 to 255, as said below
Outputs:
- master_cuts: float32 [256, 32768], P('clus', 'scen')
The draws below stay inside these ranges and needn't reach their ends.
Inputs may be any that keep to these rules, and one draw needn't show every extreme that they name: counts of live slots, one device holding 64 live slots in every draw. A permutation of the master cut rows; of the cuts k = i * 16 to (i + 1) * 16 - 1 at most 1 have cut_owner_rows[k] in e * 16 to (e + 1) * 16 - 1, for any i and e, and 1 is reached.
All inputs are finite; a program needn't handle non-finite values.
Results may differ from the reference program's by a relative error of at most 0.0029.
Values sent between devices are 32-bit elements; how exact they have to be, the bound alone decides.
A program may use at most 64 MiB of HBM per device.

```python
import math
import jax
import jax.numpy as jnp
from jax import lax

N1 = 32768
BLK = 128
KC = 16
NB = 2
SLOTS = 64
NCB = 256
GROUPS = 256
CUTS = 256
SCEN_ALL = 16384
N_CLUS = 16


def draw_counts(key, part):
    first = jax.random.fold_in(key, 11)
    second = jax.random.fold_in(key, 23)
    values = jax.random.randint(first, (GROUPS,), SLOTS // 4, SLOTS + 1)
    largest_cluster = jax.random.randint(second, (), 0, GROUPS)
    return jnp.where(jnp.arange(GROUPS) == largest_cluster, SLOTS, values).astype(jnp.int32)


def draw_cut_owner_rows(key, part):
    device_perm = jax.random.permutation(jax.random.fold_in(key, 5), N_CLUS)
    source_perm = jax.random.permutation(jax.random.fold_in(key, 9), N_CLUS)
    slot_key = jax.random.fold_in(key, 7)
    slot_table = jax.vmap(lambda e: jax.random.permutation(jax.random.fold_in(slot_key, e), KC))(jnp.arange(N_CLUS, dtype=jnp.int32))
    source = jnp.arange(CUTS, dtype=jnp.int32) // KC
    within = jnp.arange(CUTS, dtype=jnp.int32) % KC
    target = device_perm[(source_perm[source] + within) % N_CLUS]
    return (target * KC + slot_table[target, within]).astype(jnp.int32)


def plant(result, stream_key, smallest, high):
    index_at = [jax.random.randint(jax.random.fold_in(stream_key, axis), (), 0, length) for axis, length in enumerate(result.shape)]
    widest = result.shape.index(max(result.shape))
    neighbour = index_at[:widest] + [(index_at[widest] + 1) % result.shape[widest]] + index_at[widest + 1:]
    return result.at[tuple(index_at)].set(smallest).at[tuple(neighbour)].set(high)


def block_scale(rng, extent, shards, smallest, high):
    def one(axis_at, blocks):
        steps = jax.random.uniform(jax.random.fold_in(jax.random.fold_in(rng, 6), axis_at), (blocks,), jnp.float32, smallest / len(shards), high / len(shards))
        return jnp.repeat(jnp.exp(steps), extent[axis_at] // blocks).reshape((-1,) + (1,) * (len(extent) - axis_at - 1))

    level = one(*shards[0])
    for cut in shards[1:]:
        level = level * one(*cut)
    return level


def noise(rng, extent, spread, most, pieces=(), held_as=jnp.bfloat16):
    loudness = block_scale(rng, extent, pieces, -0.22, 0.18) if pieces else 1.0
    values = jax.random.normal(rng, extent, jnp.float32) * spread * loudness
    return jnp.minimum(jnp.maximum(values, -most), most).astype(held_as)


def setup_inputs(seed: int = 0) -> dict:
    streams_of = jax.random.split(jax.random.key(seed), 8)
    duals = noise(streams_of[0], (SCEN_ALL, NB, BLK), 1.0, 6.0, ((0, 256),))
    blocks = noise(streams_of[1], (SCEN_ALL, NB, BLK, BLK), BLK ** -0.5, 0.5, ((0, 256),))
    prob = jnp.clip(jnp.exp(math.log(4.0) - 2.7725887 * jax.random.uniform(streams_of[2], (SCEN_ALL,), jnp.float32) ** block_scale(streams_of[2], (SCEN_ALL,), ((0, 256),), -0.2, 0.2)), 0.25, 4.0)
    cluster_map = plant(jax.random.randint(streams_of[3], (SCEN_ALL,), 0, KC), jax.random.fold_in(streams_of[3], 1), 0, KC - 1).astype(jnp.int32)
    block_cols = plant(jax.random.randint(streams_of[4], (SCEN_ALL, NB), 0, NCB), jax.random.fold_in(streams_of[4], 1), 0, NCB - 1).astype(jnp.int32)
    counts = draw_counts(jax.random.fold_in(streams_of[7], 71), 0)
    cut_owner_rows = draw_cut_owner_rows(jax.random.fold_in(streams_of[7], 71), 0)
    return {"duals": duals, "blocks": blocks, "prob": prob, "cluster_map": cluster_map, "block_cols": block_cols, "counts": counts, "cut_owner_rows": cut_owner_rows}


def reference(duals, blocks, prob, cluster_map, block_cols, counts, cut_owner_rows):
    index = jnp.arange(SCEN_ALL, dtype=jnp.int32)
    group = index // SLOTS
    slot = index - group * SLOTS
    live = slot < counts[group]
    weight = jnp.where(live, prob, jnp.float32(0.0))
    weighted_duals = (weight[:, None, None] * duals.astype(jnp.float32)).astype(jnp.bfloat16)

    def one_group(pair):
        tiles, duty = pair
        return jnp.einsum("brc,br->bc", tiles.astype(jnp.float32), duty.astype(jnp.float32),
                          precision=lax.Precision.HIGHEST)

    dual_products = lax.map(one_group, (blocks.reshape(GROUPS, SLOTS * NB, BLK, BLK),
                                   weighted_duals.reshape(GROUPS, SLOTS * NB, BLK)))
    dual_products = dual_products.reshape(SCEN_ALL * NB, BLK)
    global_cluster = cluster_map + (group % N_CLUS) * KC
    keys = (global_cluster[:, None] * NCB + block_cols).reshape(-1).astype(jnp.int32)
    cuts = jnp.zeros((CUTS * NCB, BLK), jnp.float32).at[keys].add(dual_products).reshape(CUTS, N1)
    return jnp.zeros((CUTS, N1), jnp.float32).at[cut_owner_rows].set(cuts)
```

```python
import functools

import jax
import jax.numpy as jnp
from jax import lax
from jax.experimental import pallas as pl
from jax.experimental.pallas import tpu as pltpu
from jax.sharding import PartitionSpec as P

N1 = 32768
KC = 16
BLK = 128
ROWS = 128
SCEN = 16
CLUS = 16
OWN = 16
PIECE = 136
CHUNKS = ((96, 40), (64, 32), (32, 32), (0, 32))
MESH = pl.DeviceIdType.MESH
F32, BF16, I32 = jnp.float32, jnp.bfloat16, jnp.int32


def travels(direction, hop, chunk):
    return hop <= 3 or (hop == 4 and (chunk < 2) == (direction == 0))


def kernel(
    duals_h, blocks_h, prob_h, cmap_h, cols_h, counts_h, owners_h, owners2_h, out,
    blk, dua, prb, cmp, col, cnt, own, ownv, inv_v, inv_s, pieces, total, landed,
    small_sem, blk_sem, ring_send, ring_recv, sib_send, sib_recv, row_send, row_recv,
):
    s, i = lax.axis_index("scen"), lax.axis_index("clus")
    right, left, sibling = (s + 2) % SCEN, (s + SCEN - 2) % SCEN, s + 1 - 2 * (s % 2)
    nc = len(CHUNKS)

    smalls = [
        pltpu.make_async_copy(src, dst, small_sem.at[n])
        for n, (src, dst) in enumerate(
            ((counts_h, cnt), (owners_h, own), (prob_h, prb), (duals_h, dua), (cmap_h, cmp), (cols_h, col), (owners2_h, ownv))
        )
    ]
    for c in smalls:
        c.start()
    loads = []
    for n, (lo, rows) in enumerate(CHUNKS):
        c = pltpu.make_async_copy(blocks_h.at[pl.ds(lo, 32)], blk.at[pl.ds(lo, 32)], blk_sem.at[n])
        c.start()
        loads.append(c)

    barrier = pltpu.get_barrier_semaphore()
    for dev in (right, left, sibling):
        pl.semaphore_signal(barrier, inc=1, device_id=(dev, i), device_id_type=MESH)
    for k in range(1, CLUS):
        pl.semaphore_signal(barrier, inc=1, device_id=(s, (i + k) % CLUS), device_id_type=MESH)

    for c in smalls:
        c.wait()

    lane64 = lax.broadcasted_iota(I32, (1, 64), 1)
    weight = jnp.where(lane64 < cnt[0], prb[...], 0.0)
    spread = (lax.broadcasted_iota(I32, (ROWS, 64), 0) // 2) == lax.broadcasted_iota(I32, (ROWS, 64), 1)
    weight_col = jnp.sum(jnp.where(spread, weight, 0.0), axis=1, keepdims=True)
    weighted = (weight_col * dua[...].astype(F32)).astype(BF16).astype(F32)

    pick = (
        lax.broadcasted_iota(I32, (64, ROWS), 0) == lax.broadcasted_iota(I32, (64, ROWS), 1) // 2
    ).astype(F32).astype(BF16)
    both = jnp.dot(col[...].astype(F32).astype(BF16), pick, preferred_element_type=F32)
    cluster = jnp.dot(cmp[...].astype(F32).astype(BF16), pick, preferred_element_type=F32)
    lane = lax.broadcasted_iota(I32, (1, ROWS), 1)
    column = jnp.where(lane % 2 == 0, both[0:1], both[1:2])
    dest = jnp.zeros((1, ROWS), I32)
    cluster = cluster.astype(I32)
    for c in range(KC):
        dest = jnp.where(cluster == c, own[i * KC + c] // KC, dest)
    keys = dest.astype(F32) * 256.0 + column
    pieces[s, pl.ds(ROWS, 8), :] = jnp.broadcast_to(keys, (8, ROWS))

    def ring_copy(direction, hop, n):
        lo, rows = CHUNKS[n]
        source = (s + (SCEN - 2 * (hop - 1) if direction == 0 else 2 * (hop - 1))) % SCEN
        ref = pieces.at[source, pl.ds(lo, rows), :]
        return pltpu.make_async_remote_copy(
            src_ref=ref, dst_ref=ref,
            send_sem=ring_send.at[direction, hop - 1, n], recv_sem=ring_recv.at[direction, hop - 1, n],
            device_id=(right if direction == 0 else left, i), device_id_type=MESH,
        )

    def sib_copy(direction, hop, n):
        lo, rows = CHUNKS[n]
        source = (s + (SCEN - 2 * hop if direction == 0 else 2 * hop)) % SCEN
        ref = pieces.at[source, pl.ds(lo, rows), :]
        return pltpu.make_async_remote_copy(
            src_ref=ref, dst_ref=ref,
            send_sem=sib_send.at[direction, hop, n], recv_sem=sib_recv.at[direction, hop, n],
            device_id=(sibling, i), device_id_type=MESH,
        )

    started = []

    def start(copy):
        copy.start()
        started.append(copy)

    sub = lax.broadcasted_iota(I32, (8, BLK), 0)
    for n, (lo, rows) in enumerate(CHUNKS):
        loads[n].wait()
        for t in range(4):
            at = lo + 8 * t
            w = weighted[at : at + 8]
            lhs = jnp.concatenate([jnp.where(sub == g, w, 0.0) for g in range(8)], axis=1).astype(BF16)
            rhs = blk[at : at + 8].reshape(8 * BLK, BLK)
            pieces[s, pl.ds(at, 8), :] = jnp.dot(lhs, rhs, preferred_element_type=F32)
        if n == 0:
            pl.semaphore_wait(barrier, 3 + CLUS - 1)
        start(ring_copy(0, 1, n))
        start(ring_copy(1, 1, n))
        start(sib_copy(0, 0, n))

    total[...] = jnp.zeros_like(total)
    target = lax.broadcasted_iota(I32, (CLUS * OWN, ROWS), 0)

    def hot(source):
        key = pieces[source, pl.ds(ROWS, 1), :].astype(I32)
        cb = key % 256 - s * OWN
        t = jnp.where((cb >= 0) & (cb < OWN), key // 256 * OWN + cb, -1)
        return (target == t).astype(F32).astype(BF16)

    def add(first, second):
        onehot = jnp.concatenate([hot(first), hot(second)], axis=1)
        p = jnp.concatenate([pieces[first, pl.ds(0, ROWS), :], pieces[second, pl.ds(0, ROWS), :]], axis=0)
        high = p.astype(BF16)
        low = (p - high.astype(F32)).astype(BF16)
        total[...] += jnp.dot(onehot, high, preferred_element_type=F32) + jnp.dot(
            onehot, low, preferred_element_type=F32
        )

    def place(direction, hop, of=None):
        of = s if of is None else of
        return (of + (SCEN - 2 * hop if direction == 0 else 2 * hop)) % SCEN

    def add_hop(direction, hop):
        for n in range(nc):
            sib_copy(direction, hop, n).wait_recv()
        add(place(direction, hop), place(direction, hop, sibling))

    lane256 = lax.broadcasted_iota(I32, (16, 256), 1)
    row16 = lax.broadcasted_iota(I32, (16, 256), 0)
    ownrow = ownv[...]
    inv_col = jnp.max(jnp.where(ownrow == i * KC + row16, lane256 // KC, 0), axis=1, keepdims=True)
    inv_v[...] = jnp.broadcast_to(inv_col, (16, 128))
    c = pltpu.make_async_copy(inv_v, inv_s, small_sem.at[0])
    c.start()
    c.wait()

    for hop in range(1, 5):
        for n in range(nc):
            for direction in (0, 1):
                if travels(direction, hop, n):
                    ring_copy(direction, hop, n).wait_recv()
                    if travels(direction, hop + 1, n):
                        start(ring_copy(direction, hop + 1, n))
                    start(sib_copy(direction, hop, n))
            if n == 1:
                if hop == 1:
                    add_hop(0, 0)
                else:
                    add_hop(0, hop - 1)
            if n == 3 and hop > 1:
                add_hop(1, hop - 1)
    for n in range(nc):
        sib_copy(0 if n < 2 else 1, 4, n).wait_recv()
    add(place(0, 4), place(0, 4, sibling))

    rows_out = []
    for k in range(1, CLUS):
        e = (i + k) % CLUS
        c = pltpu.make_async_remote_copy(
            src_ref=total.at[pl.ds(e * OWN, OWN), :], dst_ref=landed.at[i],
            send_sem=row_send.at[k], recv_sem=row_recv.at[k],
            device_id=(s, e), device_id_type=MESH,
        )
        c.start()
        rows_out.append(c)
    landed[i] = total[pl.ds(i * OWN, OWN), :]
    for c in rows_out:
        c.wait_recv()
    for r in range(KC):
        row = landed[inv_s[r, 0]]
        for cb in range(OWN):
            out[pl.ds(r, 1), pl.ds(cb * BLK, BLK)] = row[cb : cb + 1]
    for c in rows_out:
        c.wait_send()
    for c in started:
        c.wait_send()


def body(duals, blocks, prob, cluster_map, block_cols, counts, cut_owner_rows):
    any_ = pl.BlockSpec(memory_space=pltpu.HBM)
    dma = pltpu.SemaphoreType.DMA
    return pl.pallas_call(
        kernel,
        out_shape=jax.ShapeDtypeStruct((KC, OWN * BLK), F32),
        in_specs=[any_] * 8,
        out_specs=pl.BlockSpec(memory_space=pltpu.VMEM),
        scratch_shapes=[
            pltpu.VMEM((ROWS, BLK, BLK), BF16),
            pltpu.VMEM((ROWS, BLK), BF16),
            pltpu.VMEM((1, 64), F32),
            pltpu.VMEM((1, 64), I32),
            pltpu.VMEM((2, 64), I32),
            pltpu.SMEM((1,), I32),
            pltpu.SMEM((256,), I32),
            pltpu.VMEM((1, 256), I32),
            pltpu.VMEM((16, 128), I32),
            pltpu.SMEM((16, 128), I32),
            pltpu.VMEM((SCEN, PIECE, BLK), F32),
            pltpu.VMEM((CLUS * OWN, BLK), F32),
            pltpu.VMEM((CLUS, OWN, BLK), F32),
            dma((8,)),
            dma((4,)),
            dma((2, 4, 4)),
            dma((2, 4, 4)),
            dma((2, 5, 4)),
            dma((2, 5, 4)),
            dma((CLUS,)),
            dma((CLUS,)),
        ],
        compiler_params=pltpu.CompilerParams(
            collective_id=0, has_side_effects=True, vmem_limit_bytes=63 << 20
        ),
    )(
        duals.reshape(ROWS, BLK),
        blocks.reshape(ROWS, BLK, BLK),
        prob.reshape(1, 64),
        cluster_map.reshape(1, 64),
        block_cols.T,
        counts,
        cut_owner_rows,
        cut_owner_rows.reshape(1, 256),
    )


def solution(mesh):
    placed = (
        P(("scen", "clus"), None, None),
        P(("scen", "clus"), None, None, None),
        P(("scen", "clus")),
        P(("scen", "clus")),
        P(("scen", "clus"), None),
        P(("scen", "clus")),
        P(),
    )
    return jax.shard_map(
        body, mesh=mesh, in_specs=placed, out_specs=P("clus", "scen"), check_vma=False
    )
```

```python
import functools

import jax
import jax.numpy as jnp
from jax import lax
from jax.experimental import pallas as pl
from jax.experimental.pallas import tpu as pltpu
from jax.sharding import PartitionSpec as P

N1 = 32768
KC = 16
BLK = 128
ROWS = 128
SCEN = 16
CLUS = 16
OWN = 16
PIECE = 136
CHUNKS = ((96, 40), (64, 32), (32, 32), (0, 32))
MESH = pl.DeviceIdType.MESH
F32, BF16, I32 = jnp.float32, jnp.bfloat16, jnp.int32


def travels(direction, hop, chunk):
    return hop <= 3 or (hop == 4 and (chunk < 2) == (direction == 0))


def kernel(
    duals_h, blocks_h, prob_h, cmap_h, cols_h, counts_h, owners_h, owners2_h, out,
    blk, dua, prb, cmp, col, cnt, own, ownv, inv_v, inv_s, pieces, total, landed,
    small_sem, blk_sem, ring_send, ring_recv, sib_send, sib_recv, row_send, row_recv,
):
    s, i = lax.axis_index("scen"), lax.axis_index("clus")
    right, left, sibling = (s + 2) % SCEN, (s + SCEN - 2) % SCEN, s + 1 - 2 * (s % 2)
    nc = len(CHUNKS)

    smalls = [
        pltpu.make_async_copy(src, dst, small_sem.at[n])
        for n, (src, dst) in enumerate(
            ((counts_h, cnt), (owners_h, own), (prob_h, prb), (duals_h, dua), (cmap_h, cmp), (cols_h, col), (owners2_h, ownv))
        )
    ]
    for c in smalls:
        c.start()
    loads = []
    for n, (lo, rows) in enumerate(CHUNKS):
        c = pltpu.make_async_copy(blocks_h.at[pl.ds(lo, 32)], blk.at[pl.ds(lo, 32)], blk_sem.at[n])
        c.start()
        loads.append(c)

    barrier = pltpu.get_barrier_semaphore()
    for dev in (right, left, sibling):
        pl.semaphore_signal(barrier, inc=1, device_id=(dev, i), device_id_type=MESH)
    for k in range(1, CLUS):
        pl.semaphore_signal(barrier, inc=1, device_id=(s, (i + k) % CLUS), device_id_type=MESH)

    for c in smalls:
        c.wait()

    lane64 = lax.broadcasted_iota(I32, (1, 64), 1)
    weight = jnp.where(lane64 < cnt[0], prb[...], 0.0)
    spread = (lax.broadcasted_iota(I32, (ROWS, 64), 0) // 2) == lax.broadcasted_iota(I32, (ROWS, 64), 1)
    weight_col = jnp.sum(jnp.where(spread, weight, 0.0), axis=1, keepdims=True)
    weighted = (weight_col * dua[...].astype(F32)).astype(BF16).astype(F32)

    pick = (
        lax.broadcasted_iota(I32, (64, ROWS), 0) == lax.broadcasted_iota(I32, (64, ROWS), 1) // 2
    ).astype(F32).astype(BF16)
    both = jnp.dot(col[...].astype(F32).astype(BF16), pick, preferred_element_type=F32)
    cluster = jnp.dot(cmp[...].astype(F32).astype(BF16), pick, preferred_element_type=F32)
    lane = lax.broadcasted_iota(I32, (1, ROWS), 1)
    column = jnp.where(lane % 2 == 0, both[0:1], both[1:2])
    dest = jnp.zeros((1, ROWS), I32)
    cluster = cluster.astype(I32)
    for c in range(KC):
        dest = jnp.where(cluster == c, own[i * KC + c] // KC, dest)
    keys = dest.astype(F32) * 256.0 + column
    pieces[s, pl.ds(ROWS, 8), :] = jnp.broadcast_to(keys, (8, ROWS))

    def ring_copy(direction, hop, n):
        lo, rows = CHUNKS[n]
        source = (s + (SCEN - 2 * (hop - 1) if direction == 0 else 2 * (hop - 1))) % SCEN
        ref = pieces.at[source, pl.ds(lo, rows), :]
        return pltpu.make_async_remote_copy(
            src_ref=ref, dst_ref=ref,
            send_sem=ring_send.at[direction, hop - 1, n], recv_sem=ring_recv.at[direction, hop - 1, n],
            device_id=(right if direction == 0 else left, i), device_id_type=MESH,
        )

    def sib_copy(direction, hop, n):
        lo, rows = CHUNKS[n]
        source = (s + (SCEN - 2 * hop if direction == 0 else 2 * hop)) % SCEN
        ref = pieces.at[source, pl.ds(lo, rows), :]
        return pltpu.make_async_remote_copy(
            src_ref=ref, dst_ref=ref,
            send_sem=sib_send.at[direction, hop, n], recv_sem=sib_recv.at[direction, hop, n],
            device_id=(sibling, i), device_id_type=MESH,
        )

    started = []

    def start(copy):
        copy.start()
        started.append(copy)

    sub = lax.broadcasted_iota(I32, (8, BLK), 0)
    for n, (lo, rows) in enumerate(CHUNKS):
        loads[n].wait()
        for t in range(4):
            at = lo + 8 * t
            w = weighted[at : at + 8]
            lhs = jnp.concatenate([jnp.where(sub == g, w, 0.0) for g in range(8)], axis=1).astype(BF16)
            rhs = blk[at : at + 8].reshape(8 * BLK, BLK)
            pieces[s, pl.ds(at, 8), :] = jnp.dot(lhs, rhs, preferred_element_type=F32)
        if n == 0:
            pl.semaphore_wait(barrier, 3 + CLUS - 1)
        start(ring_copy(0, 1, n))
        start(ring_copy(1, 1, n))
        start(sib_copy(0, 0, n))

    total[...] = jnp.zeros_like(total)
    target = lax.broadcasted_iota(I32, (CLUS * OWN, ROWS), 0)

    def hot(source):
        key = pieces[source, pl.ds(ROWS, 1), :].astype(I32)
        cb = key % 256 - s * OWN
        t = jnp.where((cb >= 0) & (cb < OWN), key // 256 * OWN + cb, -1)
        return (target == t).astype(F32).astype(BF16)

    def add(first, second):
        onehot = jnp.concatenate([hot(first), hot(second)], axis=1)
        p = jnp.concatenate([pieces[first, pl.ds(0, ROWS), :], pieces[second, pl.ds(0, ROWS), :]], axis=0)
        high = p.astype(BF16)
        low = (p - high.astype(F32)).astype(BF16)
        total[...] += jnp.dot(onehot, high, preferred_element_type=F32) + jnp.dot(
            onehot, low, preferred_element_type=F32
        )

    def place(direction, hop, of=None):
        of = s if of is None else of
        return (of + (SCEN - 2 * hop if direction == 0 else 2 * hop)) % SCEN

    def add_hop(direction, hop):
        for n in range(nc):
            sib_copy(direction, hop, n).wait_recv()
        add(place(direction, hop), place(direction, hop, sibling))

    lane256 = lax.broadcasted_iota(I32, (16, 256), 1)
    row16 = lax.broadcasted_iota(I32, (16, 256), 0)
    ownrow = ownv[...]
    inv_col = jnp.max(jnp.where(ownrow == i * KC + row16, lane256 // KC, 0), axis=1, keepdims=True)
    inv_v[...] = jnp.broadcast_to(inv_col, (16, 128))
    c = pltpu.make_async_copy(inv_v, inv_s, small_sem.at[0])
    c.start()
    c.wait()

    for hop in range(1, 5):
        for n in range(nc):
            for direction in (0, 1):
                if travels(direction, hop, n):
                    ring_copy(direction, hop, n).wait_recv()
                    if travels(direction, hop + 1, n):
                        start(ring_copy(direction, hop + 1, n))
                    start(sib_copy(direction, hop, n))
            if n == 1:
                if hop == 1:
                    add_hop(0, 0)
                else:
                    add_hop(0, hop - 1)
            if n == 3 and hop > 1:
                add_hop(1, hop - 1)
    for n in range(nc):
        sib_copy(0 if n < 2 else 1, 4, n).wait_recv()
    add(place(0, 4), place(0, 4, sibling))

    rows_out = []
    for k in range(1, CLUS):
        e = (i + k) % CLUS
        c = pltpu.make_async_remote_copy(
            src_ref=total.at[pl.ds(e * OWN, OWN), :], dst_ref=landed.at[i],
            send_sem=row_send.at[k], recv_sem=row_recv.at[k],
            device_id=(s, e), device_id_type=MESH,
        )
        c.start()
        rows_out.append(c)
    landed[i] = total[pl.ds(i * OWN, OWN), :]
    for c in rows_out:
        c.wait_recv()
    for r in range(KC):
        row = landed[inv_s[r, 0]]
        for cb in range(OWN):
            out[pl.ds(r, 1), pl.ds(cb * BLK, BLK)] = row[cb : cb + 1]
    for c in rows_out:
        c.wait_send()
    for c in started:
        c.wait_send()


CAP = 23
MSG = 24
SLOT = 32
RING = tuple((dz, dc) for dz in (4, 3, 5, 2, 6, 1, 7, 0) for dc in (0, 1) if (dz, dc) != (0, 0))
TORUS = tuple(
    sorted(
        ((dy, dx) for dy in range(4) for dx in range(4) if (dy, dx) != (0, 0)),
        key=lambda d: -(min(d[0], 4 - d[0]) + min(d[1], 4 - d[1])),
    )
)


def routed(
    duals_h, blocks_h, prob_h, cmap_h, cols_h, counts_h, owners_h, owners2_h, out, flag,
    blk, dua, prb, cmp, col, cnt, own, ownv, inv_v, inv_s, prod, msgs, landed, total, rows,
    small_sem, blk_sem, msg_send, msg_recv, row_send, row_recv,
):
    s, i = lax.axis_index("scen"), lax.axis_index("clus")
    z, c, y, x = s // 2, s % 2, i // 4, i % 4
    scen_peers = [(z + dz) % 8 * 2 + (c if dc == 0 else 1 - c) for dz, dc in RING]
    clus_peers = [(y + dy) % 4 * 4 + (x + dx) % 4 for dy, dx in TORUS]

    barrier = pltpu.get_barrier_semaphore()
    for p in scen_peers:
        pl.semaphore_signal(barrier, inc=1, device_id=(p, i), device_id_type=MESH)
    for p in clus_peers:
        pl.semaphore_signal(barrier, inc=1, device_id=(s, p), device_id_type=MESH)

    smalls = [
        pltpu.make_async_copy(src, dst, small_sem.at[n])
        for n, (src, dst) in enumerate(
            ((counts_h, cnt), (owners_h, own), (prob_h, prb), (duals_h, dua), (cmap_h, cmp), (cols_h, col), (owners2_h, ownv))
        )
    ]
    for copy in smalls:
        copy.start()
    loads = []
    for n in range(4):
        part = pl.ds(32 * n, 32)
        loads.append(pltpu.make_async_copy(blocks_h.at[part], blk.at[part], blk_sem.at[n]))
        loads[-1].start()
    for src in range(SCEN):
        landed[src, pl.ds(MSG, SLOT - MSG), :] = jnp.zeros((SLOT - MSG, BLK), F32)
    for copy in smalls:
        copy.wait()

    lane64 = lax.broadcasted_iota(I32, (1, 64), 1)
    weight = jnp.where(lane64 < cnt[0], prb[...], 0.0)
    spread = (lax.broadcasted_iota(I32, (ROWS, 64), 0) // 2) == lax.broadcasted_iota(I32, (ROWS, 64), 1)
    weight_col = jnp.sum(jnp.where(spread, weight, 0.0), axis=1, keepdims=True)
    weighted = (weight_col * dua[...].astype(F32)).astype(BF16).astype(F32)

    pick = (
        lax.broadcasted_iota(I32, (64, ROWS), 0) == lax.broadcasted_iota(I32, (64, ROWS), 1) // 2
    ).astype(F32).astype(BF16)
    both = jnp.dot(col[...].astype(F32).astype(BF16), pick, preferred_element_type=F32)
    cluster = jnp.dot(cmp[...].astype(F32).astype(BF16), pick, preferred_element_type=F32).astype(I32)
    lane = lax.broadcasted_iota(I32, (1, ROWS), 1)
    column = jnp.where(lane % 2 == 0, both[0:1], both[1:2]).astype(I32)
    live = lane // 2 < cnt[0]
    dest = jnp.zeros((1, ROWS), I32)
    for k in range(KC):
        dest = jnp.where(cluster == k, own[i * KC + k] // KC, dest)
    owner = jnp.where(live, column // OWN, -1)
    target = dest * OWN + column % OWN + 1
    mine = lax.broadcasted_iota(I32, (SCEN, ROWS), 0) == owner
    before = (
        lax.broadcasted_iota(I32, (ROWS, ROWS), 0) < lax.broadcasted_iota(I32, (ROWS, ROWS), 1)
    ).astype(F32).astype(BF16)
    ahead = jnp.dot(mine.astype(F32).astype(BF16), before, preferred_element_type=F32)
    rank = jnp.sum(jnp.where(mine, ahead, 0.0), axis=0, keepdims=True).astype(I32)
    over = jnp.max(rank, axis=1, keepdims=True) >= CAP
    slot = jnp.where(live & (rank < CAP), owner * MSG + rank, -1)
    gather = (lax.broadcasted_iota(I32, (SCEN * MSG, ROWS), 0) == slot).astype(F32).astype(BF16)
    values = jnp.where(mine & (rank < CAP), target, 0).astype(F32).astype(BF16)
    places = (
        lax.broadcasted_iota(I32, (ROWS, ROWS), 0) == rank + s % 4 * SLOT
    ).astype(F32).astype(BF16)
    keys = lax.dot_general(values, places, (((1,), (1,)), ((), ())), preferred_element_type=F32)
    keys = jnp.where(lax.broadcasted_iota(I32, (SCEN, ROWS), 1) == ROWS - 1, jnp.where(over, -1.0, 0.0), keys)

    row16 = lax.broadcasted_iota(I32, (16, 256), 0)
    lane256 = lax.broadcasted_iota(I32, (16, 256), 1)
    inv_col = jnp.max(jnp.where(ownv[...] == i * KC + row16, lane256 // KC, 0), axis=1, keepdims=True)
    inv_v[...] = jnp.broadcast_to(inv_col, (16, 128))
    inverse = pltpu.make_async_copy(inv_v, inv_s, small_sem.at[7])
    inverse.start()

    sub = lax.broadcasted_iota(I32, (8, BLK), 0)
    for t in range(ROWS // 8):
        if t % 4 == 0:
            loads[t // 4].wait()
        w = weighted[8 * t : 8 * t + 8]
        lhs = jnp.concatenate([jnp.where(sub == g, w, 0.0) for g in range(8)], axis=1).astype(BF16)
        rhs = blk[8 * t : 8 * t + 8].reshape(8 * BLK, BLK)
        prod[pl.ds(8 * t, 8), :] = jnp.dot(lhs, rhs, preferred_element_type=F32)

    def exact(onehot, values):
        high = values.astype(BF16)
        low = (values - high.astype(F32)).astype(BF16)
        return jnp.dot(onehot, high, preferred_element_type=F32) + jnp.dot(onehot, low, preferred_element_type=F32)

    sent = exact(gather, prod[...])
    for d in range(SCEN):
        msgs[d] = sent[d * MSG : (d + 1) * MSG]
    for d in range(SCEN):
        msgs[d, pl.ds(CAP, 1), :] = keys[d : d + 1]

    inverse.wait()
    pl.semaphore_wait(barrier, len(RING) + len(TORUS))

    def message(k, d, src):
        return pltpu.make_async_remote_copy(
            src_ref=msgs.at[d], dst_ref=landed.at[src, pl.ds(0, MSG), :],
            send_sem=msg_send.at[k], recv_sem=msg_recv.at[src],
            device_id=(d, i), device_id_type=MESH,
        )

    for k, p in enumerate(scen_peers):
        message(k, p, s).start()
    pltpu.make_async_copy(msgs.at[s], landed.at[s, pl.ds(0, MSG), :], msg_recv.at[s]).start()

    cell = lax.broadcasted_iota(I32, (CLUS * OWN, ROWS), 0).astype(F32) + 1.0
    least = jnp.zeros((1, ROWS), F32)
    for n, step in enumerate((0, 1, 3, 2)):
        group = (z // 2 + step) % 4 * 4
        for a in range(4):
            message(0, s, group + a).wait_recv()
        key = landed[group, pl.ds(CAP, 1), :]
        for a in range(1, 4):
            key = key + landed[group + a, pl.ds(CAP, 1), :]
        least = jnp.minimum(least, key)
        part = exact((cell == key).astype(F32).astype(BF16), landed[pl.ds(group, 4)].reshape(4 * SLOT, BLK))
        if n < 3:
            total[...] = part if n == 0 else total[...] + part
        else:
            spoilt = jnp.where(jnp.min(least, axis=1, keepdims=True) < 0.0, jnp.float32(jnp.nan), 0.0)
            total[...] = total[...] + (part + spoilt)

    def row(k, e, src):
        return pltpu.make_async_remote_copy(
            src_ref=total.at[pl.ds(e * OWN, OWN), :], dst_ref=rows.at[src],
            send_sem=row_send.at[k], recv_sem=row_recv.at[src],
            device_id=(s, e), device_id_type=MESH,
        )

    for k, p in enumerate(clus_peers):
        row(k, p, i).start()
    pltpu.make_async_copy(total.at[pl.ds(i * OWN, OWN), :], rows.at[i], row_recv.at[i]).start()
    for src in range(CLUS):
        row(0, i, src).wait_recv()
    seen = rows[0, pl.ds(0, 1), :]
    for src in range(1, CLUS):
        seen = seen + rows[src, pl.ds(0, 1), :]
    bad = jnp.max(jnp.where(seen != seen, 1, 0))
    flag[0, 0] = bad
    for r in range(KC):
        line = rows[inv_s[r, 0]]
        for cb in range(OWN):
            out[pl.ds(r, 1), pl.ds(cb * BLK, BLK)] = line[cb : cb + 1]
    for k, p in enumerate(scen_peers):
        message(k, p, s).wait_send()
    for k, p in enumerate(clus_peers):
        row(k, p, i).wait_send()


def body(duals, blocks, prob, cluster_map, block_cols, counts, cut_owner_rows):
    dma = pltpu.SemaphoreType.DMA
    arrays = (
        duals.reshape(ROWS, BLK),
        blocks.reshape(ROWS, BLK, BLK),
        prob.reshape(1, 64),
        cluster_map.reshape(1, 64),
        block_cols.T,
        counts,
        cut_owner_rows,
        cut_owner_rows.reshape(1, 256),
    )
    inputs = [
        pltpu.VMEM((ROWS, BLK, BLK), BF16),
        pltpu.VMEM((ROWS, BLK), BF16),
        pltpu.VMEM((1, 64), F32),
        pltpu.VMEM((1, 64), I32),
        pltpu.VMEM((2, 64), I32),
        pltpu.SMEM((1,), I32),
        pltpu.SMEM((256,), I32),
        pltpu.VMEM((1, 256), I32),
        pltpu.VMEM((16, 128), I32),
        pltpu.SMEM((16, 128), I32),
    ]
    block = jax.ShapeDtypeStruct((KC, OWN * BLK), F32)
    vmem = pl.BlockSpec(memory_space=pltpu.VMEM)

    def call(fn, shapes, specs, scratch, cid):
        return pl.pallas_call(
            fn,
            out_shape=shapes,
            in_specs=[pl.BlockSpec(memory_space=pltpu.HBM)] * len(arrays),
            out_specs=specs,
            scratch_shapes=inputs + scratch,
            compiler_params=pltpu.CompilerParams(
                collective_id=cid, has_side_effects=True, vmem_limit_bytes=60 << 20
            ),
        )(*arrays)

    def gathered():
        scratch = [
            pltpu.VMEM((SCEN, PIECE, BLK), F32),
            pltpu.VMEM((CLUS * OWN, BLK), F32),
            pltpu.VMEM((CLUS, OWN, BLK), F32),
            dma((8,)),
            dma((4,)),
            dma((2, 4, 4)),
            dma((2, 4, 4)),
            dma((2, 5, 4)),
            dma((2, 5, 4)),
            dma((CLUS,)),
            dma((CLUS,)),
        ]
        return call(kernel, block, vmem, scratch, 0)

    scratch = [
        pltpu.VMEM((ROWS, BLK), F32),
        pltpu.VMEM((SCEN, MSG, BLK), F32),
        pltpu.VMEM((SCEN, SLOT, BLK), F32),
        pltpu.VMEM((CLUS * OWN, BLK), F32),
        pltpu.VMEM((CLUS, OWN, BLK), F32),
        dma((8,)),
        dma((4,)),
        dma((SCEN,)),
        dma((SCEN,)),
        dma((CLUS,)),
        dma((CLUS,)),
    ]
    flag = jax.ShapeDtypeStruct((1, 1), I32)
    out, full = call(routed, (block, flag), (vmem, pl.BlockSpec(memory_space=pltpu.SMEM)), scratch, 1)
    return lax.cond(full[0, 0] != 0, gathered, lambda: out)


def solution(mesh):
    placed = (
        P(("scen", "clus"), None, None),
        P(("scen", "clus"), None, None, None),
        P(("scen", "clus")),
        P(("scen", "clus")),
        P(("scen", "clus"), None),
        P(("scen", "clus")),
        P(),
    )
    return jax.shard_map(
        body, mesh=mesh, in_specs=placed, out_specs=P("clus", "scen"), check_vma=False
    )
```

```python
import functools

import jax
import jax.numpy as jnp
from jax import lax
from jax.experimental import pallas as pl
from jax.experimental.pallas import tpu as pltpu
from jax.sharding import PartitionSpec as P

N1 = 32768
KC = 16
BLK = 128
ROWS = 128
SCEN = 16
CLUS = 16
OWN = 16
PIECE = 136
CHUNKS = ((96, 40), (64, 32), (32, 32), (0, 32))
MESH = pl.DeviceIdType.MESH
F32, BF16, I32 = jnp.float32, jnp.bfloat16, jnp.int32


def travels(direction, hop, chunk):
    return hop <= 3 or (hop == 4 and (chunk < 2) == (direction == 0))


def kernel(
    duals_h, blocks_h, prob_h, cmap_h, cols_h, counts_h, owners_h, owners2_h, out,
    blk, dua, prb, cmp, col, cnt, own, ownv, inv_v, inv_s, pieces, total, landed,
    small_sem, blk_sem, ring_send, ring_recv, sib_send, sib_recv, row_send, row_recv,
):
    s, i = lax.axis_index("scen"), lax.axis_index("clus")
    right, left, sibling = (s + 2) % SCEN, (s + SCEN - 2) % SCEN, s + 1 - 2 * (s % 2)
    nc = len(CHUNKS)

    smalls = [
        pltpu.make_async_copy(src, dst, small_sem.at[n])
        for n, (src, dst) in enumerate(
            ((counts_h, cnt), (owners_h, own), (prob_h, prb), (duals_h, dua), (cmap_h, cmp), (cols_h, col), (owners2_h, ownv))
        )
    ]
    for c in smalls:
        c.start()
    loads = []
    for n, (lo, rows) in enumerate(CHUNKS):
        c = pltpu.make_async_copy(blocks_h.at[pl.ds(lo, 32)], blk.at[pl.ds(lo, 32)], blk_sem.at[n])
        c.start()
        loads.append(c)

    barrier = pltpu.get_barrier_semaphore()
    for dev in (right, left, sibling):
        pl.semaphore_signal(barrier, inc=1, device_id=(dev, i), device_id_type=MESH)
    for k in range(1, CLUS):
        pl.semaphore_signal(barrier, inc=1, device_id=(s, (i + k) % CLUS), device_id_type=MESH)

    for c in smalls:
        c.wait()

    lane64 = lax.broadcasted_iota(I32, (1, 64), 1)
    weight = jnp.where(lane64 < cnt[0, 0], prb[...], 0.0)
    spread = (lax.broadcasted_iota(I32, (ROWS, 64), 0) // 2) == lax.broadcasted_iota(I32, (ROWS, 64), 1)
    weight_col = jnp.sum(jnp.where(spread, weight, 0.0), axis=1, keepdims=True)
    weighted = (weight_col * dua[...].astype(F32)).astype(BF16).astype(F32)

    pick = (
        lax.broadcasted_iota(I32, (64, ROWS), 0) == lax.broadcasted_iota(I32, (64, ROWS), 1) // 2
    ).astype(F32).astype(BF16)
    both = jnp.dot(col[...].astype(F32).astype(BF16), pick, preferred_element_type=F32)
    cluster = jnp.dot(cmp[...].astype(F32).astype(BF16), pick, preferred_element_type=F32)
    lane = lax.broadcasted_iota(I32, (1, ROWS), 1)
    column = jnp.where(lane % 2 == 0, both[0:1], both[1:2])
    dest = jnp.zeros((1, ROWS), I32)
    cluster = cluster.astype(I32)
    for c in range(KC):
        dest = jnp.where(cluster == c, own[i * KC + c] // KC, dest)
    keys = dest.astype(F32) * 256.0 + column
    pieces[s, pl.ds(ROWS, 8), :] = jnp.broadcast_to(keys, (8, ROWS))

    def ring_copy(direction, hop, n):
        lo, rows = CHUNKS[n]
        source = (s + (SCEN - 2 * (hop - 1) if direction == 0 else 2 * (hop - 1))) % SCEN
        ref = pieces.at[source, pl.ds(lo, rows), :]
        return pltpu.make_async_remote_copy(
            src_ref=ref, dst_ref=ref,
            send_sem=ring_send.at[direction, hop - 1, n], recv_sem=ring_recv.at[direction, hop - 1, n],
            device_id=(right if direction == 0 else left, i), device_id_type=MESH,
        )

    def sib_copy(direction, hop, n):
        lo, rows = CHUNKS[n]
        source = (s + (SCEN - 2 * hop if direction == 0 else 2 * hop)) % SCEN
        ref = pieces.at[source, pl.ds(lo, rows), :]
        return pltpu.make_async_remote_copy(
            src_ref=ref, dst_ref=ref,
            send_sem=sib_send.at[direction, hop, n], recv_sem=sib_recv.at[direction, hop, n],
            device_id=(sibling, i), device_id_type=MESH,
        )

    started = []

    def start(copy):
        copy.start()
        started.append(copy)

    sub = lax.broadcasted_iota(I32, (8, BLK), 0)
    for n, (lo, rows) in enumerate(CHUNKS):
        loads[n].wait()
        for t in range(4):
            at = lo + 8 * t
            w = weighted[at : at + 8]
            lhs = jnp.concatenate([jnp.where(sub == g, w, 0.0) for g in range(8)], axis=1).astype(BF16)
            rhs = blk[at : at + 8].reshape(8 * BLK, BLK)
            pieces[s, pl.ds(at, 8), :] = jnp.dot(lhs, rhs, preferred_element_type=F32)
        if n == 0:
            pl.semaphore_wait(barrier, 3 + CLUS - 1)
        start(ring_copy(0, 1, n))
        start(ring_copy(1, 1, n))
        start(sib_copy(0, 0, n))

    total[...] = jnp.zeros_like(total)
    target = lax.broadcasted_iota(I32, (CLUS * OWN, ROWS), 0)

    def hot(source):
        key = pieces[source, pl.ds(ROWS, 1), :].astype(I32)
        cb = key % 256 - s * OWN
        t = jnp.where((cb >= 0) & (cb < OWN), key // 256 * OWN + cb, -1)
        return (target == t).astype(F32).astype(BF16)

    def add(first, second):
        onehot = jnp.concatenate([hot(first), hot(second)], axis=1)
        p = jnp.concatenate([pieces[first, pl.ds(0, ROWS), :], pieces[second, pl.ds(0, ROWS), :]], axis=0)
        high = p.astype(BF16)
        low = (p - high.astype(F32)).astype(BF16)
        total[...] += jnp.dot(onehot, high, preferred_element_type=F32) + jnp.dot(
            onehot, low, preferred_element_type=F32
        )

    def place(direction, hop, of=None):
        of = s if of is None else of
        return (of + (SCEN - 2 * hop if direction == 0 else 2 * hop)) % SCEN

    def add_hop(direction, hop):
        for n in range(nc):
            sib_copy(direction, hop, n).wait_recv()
        add(place(direction, hop), place(direction, hop, sibling))

    lane256 = lax.broadcasted_iota(I32, (16, 256), 1)
    row16 = lax.broadcasted_iota(I32, (16, 256), 0)
    ownrow = ownv[...]
    inv_col = jnp.max(jnp.where(ownrow == i * KC + row16, lane256 // KC, 0), axis=1, keepdims=True)
    inv_v[...] = jnp.broadcast_to(inv_col, (16, 128))
    c = pltpu.make_async_copy(inv_v, inv_s, small_sem.at[0])
    c.start()
    c.wait()

    for hop in range(1, 5):
        for n in range(nc):
            for direction in (0, 1):
                if travels(direction, hop, n):
                    ring_copy(direction, hop, n).wait_recv()
                    if travels(direction, hop + 1, n):
                        start(ring_copy(direction, hop + 1, n))
                    start(sib_copy(direction, hop, n))
            if n == 1:
                if hop == 1:
                    add_hop(0, 0)
                else:
                    add_hop(0, hop - 1)
            if n == 3 and hop > 1:
                add_hop(1, hop - 1)
    for n in range(nc):
        sib_copy(0 if n < 2 else 1, 4, n).wait_recv()
    add(place(0, 4), place(0, 4, sibling))

    rows_out = []
    for k in range(1, CLUS):
        e = (i + k) % CLUS
        c = pltpu.make_async_remote_copy(
            src_ref=total.at[pl.ds(e * OWN, OWN), :], dst_ref=landed.at[i],
            send_sem=row_send.at[k], recv_sem=row_recv.at[k],
            device_id=(s, e), device_id_type=MESH,
        )
        c.start()
        rows_out.append(c)
    landed[i] = total[pl.ds(i * OWN, OWN), :]
    for c in rows_out:
        c.wait_recv()
    for r in range(KC):
        row = landed[inv_s[r, 0]]
        for cb in range(OWN):
            out[pl.ds(r, 1), pl.ds(cb * BLK, BLK)] = row[cb : cb + 1]
    for c in rows_out:
        c.wait_send()
    for c in started:
        c.wait_send()


CAP = 23
MSG = 24
SLOT = 32
RING = tuple((dz, dc) for dz in (4, 3, 5, 2, 6, 1, 7, 0) for dc in (0, 1) if (dz, dc) != (0, 0))
TORUS = tuple(
    sorted(
        ((dy, dx) for dy in range(4) for dx in range(4) if (dy, dx) != (0, 0)),
        key=lambda d: -(min(d[0], 4 - d[0]) + min(d[1], 4 - d[1])),
    )
)


def routed(
    duals_h, blocks_h, prob_h, cmap_h, cols_h, counts_h, owners_h, owners2_h, out, flag,
    blk, dua, prb, cmp, col, cnt, own, ownv, inv_v, inv_s, prod, msgs, landed, total, rows,
    small_sem, blk_sem, msg_send, msg_recv, row_send, row_recv,
):
    s, i = lax.axis_index("scen"), lax.axis_index("clus")
    z, c, y, x = s // 2, s % 2, i // 4, i % 4
    scen_peers = [(z + dz) % 8 * 2 + (c if dc == 0 else 1 - c) for dz, dc in RING]
    clus_peers = [(y + dy) % 4 * 4 + (x + dx) % 4 for dy, dx in TORUS]

    barrier = pltpu.get_barrier_semaphore()
    for p in scen_peers:
        pl.semaphore_signal(barrier, inc=1, device_id=(p, i), device_id_type=MESH)

    smalls = [
        pltpu.make_async_copy(src, dst, small_sem.at[n])
        for n, (src, dst) in enumerate(
            ((counts_h, cnt), (owners_h, own), (prob_h, prb), (duals_h, dua), (cmap_h, cmp), (cols_h, col), (owners2_h, ownv))
        )
    ]
    for copy in smalls:
        copy.start()
    loads = []
    for n in range(4):
        part = pl.ds(32 * n, 32)
        loads.append(pltpu.make_async_copy(blocks_h.at[part], blk.at[part], blk_sem.at[n]))
        loads[-1].start()

    for p in clus_peers:
        pl.semaphore_signal(barrier, inc=1, device_id=(s, p), device_id_type=MESH)

    for src in range(SCEN):
        landed[src, pl.ds(MSG, SLOT - MSG), :] = jnp.zeros((SLOT - MSG, BLK), F32)
    for copy in smalls:
        copy.wait()

    lane64 = lax.broadcasted_iota(I32, (1, 64), 1)
    weight = jnp.where(lane64 < cnt[0, 0], prb[...], 0.0)
    spread = (lax.broadcasted_iota(I32, (ROWS, 64), 0) // 2) == lax.broadcasted_iota(I32, (ROWS, 64), 1)
    weight_col = jnp.sum(jnp.where(spread, weight, 0.0), axis=1, keepdims=True)
    weighted = (weight_col * dua[...].astype(F32)).astype(BF16).astype(F32)

    pick = (
        lax.broadcasted_iota(I32, (64, ROWS), 0) == lax.broadcasted_iota(I32, (64, ROWS), 1) // 2
    ).astype(F32).astype(BF16)
    both = jnp.dot(col[...].astype(F32).astype(BF16), pick, preferred_element_type=F32)
    cluster = jnp.dot(cmp[...].astype(F32).astype(BF16), pick, preferred_element_type=F32).astype(I32)
    lane = lax.broadcasted_iota(I32, (1, ROWS), 1)
    column = jnp.where(lane % 2 == 0, both[0:1], both[1:2]).astype(I32)
    live = lane // 2 < cnt[0, 0]
    dest = jnp.zeros((1, ROWS), I32)
    for k in range(KC):
        dest = jnp.where(cluster == k, own[i * KC + k] // KC, dest)
    owner = jnp.where(live, column // OWN, -1)
    target = dest * OWN + column % OWN + 1
    mine = lax.broadcasted_iota(I32, (SCEN, ROWS), 0) == owner
    before = (
        lax.broadcasted_iota(I32, (ROWS, ROWS), 0) < lax.broadcasted_iota(I32, (ROWS, ROWS), 1)
    ).astype(F32).astype(BF16)
    ahead = jnp.dot(mine.astype(F32).astype(BF16), before, preferred_element_type=F32)
    rank = jnp.sum(jnp.where(mine, ahead, 0.0), axis=0, keepdims=True).astype(I32)
    over = jnp.max(rank, axis=1, keepdims=True) >= CAP
    slot = jnp.where(live & (rank < CAP), owner * MSG + rank, -1)
    gather = (lax.broadcasted_iota(I32, (SCEN * MSG, ROWS), 0) == slot).astype(F32).astype(BF16)
    values = jnp.where(mine & (rank < CAP), target, 0).astype(F32).astype(BF16)
    places = (
        lax.broadcasted_iota(I32, (ROWS, ROWS), 0) == rank + s % 4 * SLOT
    ).astype(F32).astype(BF16)
    keys = lax.dot_general(values, places, (((1,), (1,)), ((), ())), preferred_element_type=F32)
    keys = jnp.where(lax.broadcasted_iota(I32, (SCEN, ROWS), 1) == ROWS - 1, jnp.where(over, -1.0, 0.0), keys)

    row16 = lax.broadcasted_iota(I32, (16, 256), 0)
    lane256 = lax.broadcasted_iota(I32, (16, 256), 1)
    inv_col = jnp.max(jnp.where(ownv[...] == i * KC + row16, lane256 // KC, 0), axis=1, keepdims=True)
    inv_v[...] = jnp.broadcast_to(inv_col, (16, 128))
    inverse = pltpu.make_async_copy(inv_v, inv_s, small_sem.at[7])
    inverse.start()

    sub = lax.broadcasted_iota(I32, (8, BLK), 0)
    for t in range(ROWS // 8):
        if t % 4 == 0:
            loads[t // 4].wait()
        w = weighted[8 * t : 8 * t + 8]
        lhs = jnp.concatenate([jnp.where(sub == g, w, 0.0) for g in range(8)], axis=1).astype(BF16)
        rhs = blk[8 * t : 8 * t + 8].reshape(8 * BLK, BLK)
        prod[pl.ds(8 * t, 8), :] = jnp.dot(lhs, rhs, preferred_element_type=F32)

    def exact(onehot, values):
        high = values.astype(BF16)
        low = (values - high.astype(F32)).astype(BF16)
        return jnp.dot(onehot, high, preferred_element_type=F32) + jnp.dot(onehot, low, preferred_element_type=F32)

    sent = exact(gather, prod[...])
    for d in range(SCEN):
        msgs[d] = sent[d * MSG : (d + 1) * MSG]
    for d in range(SCEN):
        msgs[d, pl.ds(CAP, 1), :] = keys[d : d + 1]

    inverse.wait()
    pl.semaphore_wait(barrier, len(RING) + len(TORUS))

    def message(k, d, src):
        return pltpu.make_async_remote_copy(
            src_ref=msgs.at[d], dst_ref=landed.at[src, pl.ds(0, MSG), :],
            send_sem=msg_send.at[k], recv_sem=msg_recv.at[src],
            device_id=(d, i), device_id_type=MESH,
        )

    for k, p in enumerate(scen_peers):
        message(k, p, s).start()
    pltpu.make_async_copy(msgs.at[s], landed.at[s, pl.ds(0, MSG), :], msg_recv.at[s]).start()

    cell = lax.broadcasted_iota(I32, (CLUS * OWN, ROWS), 0).astype(F32) + 1.0
    least = jnp.zeros((1, ROWS), F32)
    for n, step in enumerate((0, 1, 3, 2)):
        group = (z // 2 + step) % 4 * 4
        for a in range(4):
            message(0, s, group + a).wait_recv()
        key = landed[group, pl.ds(CAP, 1), :]
        for a in range(1, 4):
            key = key + landed[group + a, pl.ds(CAP, 1), :]
        least = jnp.minimum(least, key)
        part = exact((cell == key).astype(F32).astype(BF16), landed[pl.ds(group, 4)].reshape(4 * SLOT, BLK))
        if n < 3:
            total[...] = part if n == 0 else total[...] + part
        else:
            spoilt = jnp.where(jnp.min(least, axis=1, keepdims=True) < 0.0, jnp.float32(jnp.nan), 0.0)
            total[...] = total[...] + (part + spoilt)

    def row(k, e, src):
        return pltpu.make_async_remote_copy(
            src_ref=total.at[pl.ds(e * OWN, OWN), :], dst_ref=rows.at[src],
            send_sem=row_send.at[k], recv_sem=row_recv.at[src],
            device_id=(s, e), device_id_type=MESH,
        )

    for k, p in enumerate(clus_peers):
        row(k, p, i).start()
    pltpu.make_async_copy(total.at[pl.ds(i * OWN, OWN), :], rows.at[i], row_recv.at[i]).start()
    for src in range(CLUS):
        row(0, i, src).wait_recv()
    seen = rows[0, pl.ds(0, 1), :]
    for src in range(1, CLUS):
        seen = seen + rows[src, pl.ds(0, 1), :]
    bad = jnp.max(jnp.where(seen != seen, 1, 0))
    flag[0, 0] = bad
    for r in range(KC):
        line = rows[inv_s[r, 0]]
        for cb in range(OWN):
            out[pl.ds(r, 1), pl.ds(cb * BLK, BLK)] = line[cb : cb + 1]
    for k, p in enumerate(scen_peers):
        message(k, p, s).wait_send()
    for k, p in enumerate(clus_peers):
        row(k, p, i).wait_send()


def body(duals, blocks, prob, cluster_map, block_cols, counts, cut_owner_rows):
    dma = pltpu.SemaphoreType.DMA
    arrays = (
        duals.reshape(ROWS, BLK),
        blocks.reshape(ROWS, BLK, BLK),
        prob.reshape(1, 64),
        cluster_map.reshape(1, 64),
        block_cols.T,
        counts.reshape(1, 1),
        cut_owner_rows,
        cut_owner_rows.reshape(1, 256),
    )
    inputs = [
        pltpu.VMEM((ROWS, BLK, BLK), BF16),
        pltpu.VMEM((ROWS, BLK), BF16),
        pltpu.VMEM((1, 64), F32),
        pltpu.VMEM((1, 64), I32),
        pltpu.VMEM((2, 64), I32),
        pltpu.SMEM((1, 1), I32),
        pltpu.SMEM((256,), I32),
        pltpu.VMEM((1, 256), I32),
        pltpu.VMEM((16, 128), I32),
        pltpu.SMEM((16, 128), I32),
    ]
    block = pltpu.VMEM((KC, OWN * BLK), F32)
    vmem = pl.BlockSpec(memory_space=pltpu.VMEM)

    def call(fn, shapes, specs, scratch, cid):
        return pl.pallas_call(
            fn,
            out_shape=shapes,
            in_specs=[pl.BlockSpec(memory_space=pltpu.HBM)] * len(arrays),
            out_specs=specs,
            scratch_shapes=inputs + scratch,
            compiler_params=pltpu.CompilerParams(
                collective_id=cid, has_side_effects=True, vmem_limit_bytes=60 << 20
            ),
        )(*arrays)

    def gathered():
        scratch = [
            pltpu.VMEM((SCEN, PIECE, BLK), F32),
            pltpu.VMEM((CLUS * OWN, BLK), F32),
            pltpu.VMEM((CLUS, OWN, BLK), F32),
            dma((8,)),
            dma((4,)),
            dma((2, 4, 4)),
            dma((2, 4, 4)),
            dma((2, 5, 4)),
            dma((2, 5, 4)),
            dma((CLUS,)),
            dma((CLUS,)),
        ]
        return call(kernel, block, vmem, scratch, 0)

    scratch = [
        pltpu.VMEM((ROWS, BLK), F32),
        pltpu.VMEM((SCEN, MSG, BLK), F32),
        pltpu.VMEM((SCEN, SLOT, BLK), F32),
        pltpu.VMEM((CLUS * OWN, BLK), F32),
        pltpu.VMEM((CLUS, OWN, BLK), F32),
        dma((8,)),
        dma((4,)),
        dma((SCEN,)),
        dma((SCEN,)),
        dma((CLUS,)),
        dma((CLUS,)),
    ]
    flag = pltpu.SMEM((1, 1), I32)
    out, full = call(routed, (block, flag), (vmem, pl.BlockSpec(memory_space=pltpu.SMEM)), scratch, 1)
    return lax.switch(full[0, 0], (lambda: out, gathered))


def solution(mesh):
    placed = (
        P(("scen", "clus"), None, None),
        P(("scen", "clus"), None, None, None),
        P(("scen", "clus")),
        P(("scen", "clus")),
        P(("scen", "clus"), None),
        P(("scen", "clus")),
        P(),
    )
    return jax.shard_map(
        body, mesh=mesh, in_specs=placed, out_specs=P("clus", "scen"), check_vma=False
    )
```

```python
import functools

import jax
import jax.numpy as jnp
from jax import lax
from jax.experimental import pallas as pl
from jax.experimental.pallas import tpu as pltpu
from jax.sharding import PartitionSpec as P

N1 = 32768
KC = 16
BLK = 128
ROWS = 128
SCEN = 16
CLUS = 16
OWN = 16
PIECE = 136
CHUNKS = ((96, 40), (64, 32), (32, 32), (0, 32))
MESH = pl.DeviceIdType.MESH
F32, BF16, I32 = jnp.float32, jnp.bfloat16, jnp.int32


def travels(direction, hop, chunk):
    return hop <= 3 or (hop == 4 and (chunk < 2) == (direction == 0))


def kernel(
    duals_h, blocks_h, prob_h, cmap_h, cols_h, counts_h, owners_h, owners2_h, out,
    blk, dua, prb, cmp, col, cnt, own, ownv, inv_v, inv_s, pieces, total, landed,
    small_sem, blk_sem, ring_send, ring_recv, sib_send, sib_recv, row_send, row_recv,
):
    s, i = lax.axis_index("scen"), lax.axis_index("clus")
    right, left, sibling = (s + 2) % SCEN, (s + SCEN - 2) % SCEN, s + 1 - 2 * (s % 2)
    nc = len(CHUNKS)

    smalls = [
        pltpu.make_async_copy(src, dst, small_sem.at[n])
        for n, (src, dst) in enumerate(
            ((counts_h, cnt), (owners_h, own), (prob_h, prb), (duals_h, dua), (cmap_h, cmp), (cols_h, col), (owners2_h, ownv))
        )
    ]
    for c in smalls:
        c.start()
    loads = []
    for n, (lo, rows) in enumerate(CHUNKS):
        c = pltpu.make_async_copy(blocks_h.at[pl.ds(lo, 32)], blk.at[pl.ds(lo, 32)], blk_sem.at[n])
        c.start()
        loads.append(c)

    barrier = pltpu.get_barrier_semaphore()
    for dev in (right, left, sibling):
        pl.semaphore_signal(barrier, inc=1, device_id=(dev, i), device_id_type=MESH)
    for k in range(1, CLUS):
        pl.semaphore_signal(barrier, inc=1, device_id=(s, (i + k) % CLUS), device_id_type=MESH)

    for c in smalls:
        c.wait()

    lane64 = lax.broadcasted_iota(I32, (1, 64), 1)
    weight = jnp.where(lane64 < cnt[0, 0], prb[...], 0.0)
    spread = (lax.broadcasted_iota(I32, (ROWS, 64), 0) // 2) == lax.broadcasted_iota(I32, (ROWS, 64), 1)
    weight_col = jnp.sum(jnp.where(spread, weight, 0.0), axis=1, keepdims=True)
    weighted = (weight_col * dua[...].astype(F32)).astype(BF16).astype(F32)

    pick = (
        lax.broadcasted_iota(I32, (64, ROWS), 0) == lax.broadcasted_iota(I32, (64, ROWS), 1) // 2
    ).astype(F32).astype(BF16)
    both = jnp.dot(col[...].astype(F32).astype(BF16), pick, preferred_element_type=F32)
    cluster = jnp.dot(cmp[...].astype(F32).astype(BF16), pick, preferred_element_type=F32)
    lane = lax.broadcasted_iota(I32, (1, ROWS), 1)
    column = jnp.where(lane % 2 == 0, both[0:1], both[1:2])
    dest = jnp.zeros((1, ROWS), I32)
    cluster = cluster.astype(I32)
    for c in range(KC):
        dest = jnp.where(cluster == c, own[i * KC + c] // KC, dest)
    keys = dest.astype(F32) * 256.0 + column
    pieces[s, pl.ds(ROWS, 8), :] = jnp.broadcast_to(keys, (8, ROWS))

    def ring_copy(direction, hop, n):
        lo, rows = CHUNKS[n]
        source = (s + (SCEN - 2 * (hop - 1) if direction == 0 else 2 * (hop - 1))) % SCEN
        ref = pieces.at[source, pl.ds(lo, rows), :]
        return pltpu.make_async_remote_copy(
            src_ref=ref, dst_ref=ref,
            send_sem=ring_send.at[direction, hop - 1, n], recv_sem=ring_recv.at[direction, hop - 1, n],
            device_id=(right if direction == 0 else left, i), device_id_type=MESH,
        )

    def sib_copy(direction, hop, n):
        lo, rows = CHUNKS[n]
        source = (s + (SCEN - 2 * hop if direction == 0 else 2 * hop)) % SCEN
        ref = pieces.at[source, pl.ds(lo, rows), :]
        return pltpu.make_async_remote_copy(
            src_ref=ref, dst_ref=ref,
            send_sem=sib_send.at[direction, hop, n], recv_sem=sib_recv.at[direction, hop, n],
            device_id=(sibling, i), device_id_type=MESH,
        )

    started = []

    def start(copy):
        copy.start()
        started.append(copy)

    sub = lax.broadcasted_iota(I32, (8, BLK), 0)
    for n, (lo, rows) in enumerate(CHUNKS):
        loads[n].wait()
        for t in range(4):
            at = lo + 8 * t
            w = weighted[at : at + 8]
            lhs = jnp.concatenate([jnp.where(sub == g, w, 0.0) for g in range(8)], axis=1).astype(BF16)
            rhs = blk[at : at + 8].reshape(8 * BLK, BLK)
            pieces[s, pl.ds(at, 8), :] = jnp.dot(lhs, rhs, preferred_element_type=F32)
        if n == 0:
            pl.semaphore_wait(barrier, 3 + CLUS - 1)
        start(ring_copy(0, 1, n))
        start(ring_copy(1, 1, n))
        start(sib_copy(0, 0, n))

    total[...] = jnp.zeros_like(total)
    target = lax.broadcasted_iota(I32, (CLUS * OWN, ROWS), 0)

    def hot(source):
        key = pieces[source, pl.ds(ROWS, 1), :].astype(I32)
        cb = key % 256 - s * OWN
        t = jnp.where((cb >= 0) & (cb < OWN), key // 256 * OWN + cb, -1)
        return (target == t).astype(F32).astype(BF16)

    def add(first, second):
        onehot = jnp.concatenate([hot(first), hot(second)], axis=1)
        p = jnp.concatenate([pieces[first, pl.ds(0, ROWS), :], pieces[second, pl.ds(0, ROWS), :]], axis=0)
        high = p.astype(BF16)
        low = (p - high.astype(F32)).astype(BF16)
        total[...] += jnp.dot(onehot, high, preferred_element_type=F32) + jnp.dot(
            onehot, low, preferred_element_type=F32
        )

    def place(direction, hop, of=None):
        of = s if of is None else of
        return (of + (SCEN - 2 * hop if direction == 0 else 2 * hop)) % SCEN

    def add_hop(direction, hop):
        for n in range(nc):
            sib_copy(direction, hop, n).wait_recv()
        add(place(direction, hop), place(direction, hop, sibling))

    lane256 = lax.broadcasted_iota(I32, (16, 256), 1)
    row16 = lax.broadcasted_iota(I32, (16, 256), 0)
    ownrow = ownv[...]
    inv_col = jnp.max(jnp.where(ownrow == i * KC + row16, lane256 // KC, 0), axis=1, keepdims=True)
    inv_v[...] = jnp.broadcast_to(inv_col, (16, 128))
    c = pltpu.make_async_copy(inv_v, inv_s, small_sem.at[0])
    c.start()
    c.wait()

    for hop in range(1, 5):
        for n in range(nc):
            for direction in (0, 1):
                if travels(direction, hop, n):
                    ring_copy(direction, hop, n).wait_recv()
                    if travels(direction, hop + 1, n):
                        start(ring_copy(direction, hop + 1, n))
                    start(sib_copy(direction, hop, n))
            if n == 1:
                if hop == 1:
                    add_hop(0, 0)
                else:
                    add_hop(0, hop - 1)
            if n == 3 and hop > 1:
                add_hop(1, hop - 1)
    for n in range(nc):
        sib_copy(0 if n < 2 else 1, 4, n).wait_recv()
    add(place(0, 4), place(0, 4, sibling))

    rows_out = []
    for k in range(1, CLUS):
        e = (i + k) % CLUS
        c = pltpu.make_async_remote_copy(
            src_ref=total.at[pl.ds(e * OWN, OWN), :], dst_ref=landed.at[i],
            send_sem=row_send.at[k], recv_sem=row_recv.at[k],
            device_id=(s, e), device_id_type=MESH,
        )
        c.start()
        rows_out.append(c)
    landed[i] = total[pl.ds(i * OWN, OWN), :]
    for c in rows_out:
        c.wait_recv()
    for r in range(KC):
        row = landed[inv_s[r, 0]]
        for cb in range(OWN):
            out[pl.ds(r, 1), pl.ds(cb * BLK, BLK)] = row[cb : cb + 1]
    for c in rows_out:
        c.wait_send()
    for c in started:
        c.wait_send()


CAP = 15
MSG = 16
SPARE = 7
PACK = 8
RING = tuple((dz, dc) for dz in (4, 3, 5, 2, 6, 1, 7, 0) for dc in (0, 1) if (dz, dc) != (0, 0))
TORUS = tuple(
    sorted(
        ((dy, dx) for dy in range(4) for dx in range(4) if (dy, dx) != (0, 0)),
        key=lambda d: -(min(d[0], 4 - d[0]) + min(d[1], 4 - d[1])),
    )
)


def routed(
    duals_h, blocks_h, prob_h, cmap_h, cols_h, counts_h, owners_h, owners2_h, out, flag,
    blk, dua, prb, cmp, col, cnt, own, ownv, inv_v, inv_s, prod, msgs, landed, total, rows,
    pack1, pack2, spare1, spare2, late,
    small_sem, blk_sem, msg_send, msg_recv, row_send, row_recv, first_send, first_recv, second_send, second_recv,
):
    s, i = lax.axis_index("scen"), lax.axis_index("clus")
    z, c, y, x = s // 2, s % 2, i // 4, i % 4
    scen_peers = [(z + dz) % 8 * 2 + (c if dc == 0 else 1 - c) for dz, dc in RING]
    clus_peers = [(y + dy) % 4 * 4 + (x + dx) % 4 for dy, dx in TORUS]

    smalls = [
        pltpu.make_async_copy(src, dst, small_sem.at[n])
        for n, (src, dst) in enumerate(
            ((counts_h, cnt), (owners_h, own), (prob_h, prb), (duals_h, dua), (cmap_h, cmp), (cols_h, col), (owners2_h, ownv))
        )
    ]
    for copy in smalls:
        copy.start()
    loads = []
    for n, (at, many) in enumerate(((0, 64), (64, 64))):
        part = pl.ds(at, many)
        loads.append(pltpu.make_async_copy(blocks_h.at[part], blk.at[part], blk_sem.at[n]))
        loads[-1].start()


    barrier = pltpu.get_barrier_semaphore()
    for p in scen_peers:
        pl.semaphore_signal(barrier, inc=1, device_id=(p, i), device_id_type=MESH)

    for p in clus_peers:
        pl.semaphore_signal(barrier, inc=1, device_id=(s, p), device_id_type=MESH)

    for copy in smalls:
        copy.wait()

    lane64 = lax.broadcasted_iota(I32, (1, 64), 1)
    weight = jnp.where(lane64 < cnt[0, 0], prb[...], 0.0)
    spread = (lax.broadcasted_iota(I32, (ROWS, 64), 0) // 2) == lax.broadcasted_iota(I32, (ROWS, 64), 1)
    weight_col = jnp.sum(jnp.where(spread, weight, 0.0), axis=1, keepdims=True)
    weighted = (weight_col * dua[...].astype(F32)).astype(BF16).astype(F32)

    def as_bf16(mask):
        return mask.astype(F32).astype(BF16)

    pick = as_bf16(lax.broadcasted_iota(I32, (64, ROWS), 0) == lax.broadcasted_iota(I32, (64, ROWS), 1) // 2)
    both = jnp.dot(col[...].astype(F32).astype(BF16), pick, preferred_element_type=F32)
    cluster = jnp.dot(cmp[...].astype(F32).astype(BF16), pick, preferred_element_type=F32).astype(I32)
    lane = lax.broadcasted_iota(I32, (1, ROWS), 1)
    column = jnp.where(lane % 2 == 0, both[0:1], both[1:2]).astype(I32)
    live = lane // 2 < cnt[0, 0]
    dest = jnp.zeros((1, ROWS), I32)
    for k in range(KC):
        dest = jnp.where(cluster == k, own[i * KC + k] // KC, dest)
    owner = jnp.where(live, column // OWN, -1)
    target = dest * OWN + column % OWN
    mine = lax.broadcasted_iota(I32, (SCEN, ROWS), 0) == owner
    sublane = lax.broadcasted_iota(I32, (ROWS, ROWS), 0)
    before = as_bf16(sublane < lax.broadcasted_iota(I32, (ROWS, ROWS), 1))
    ahead = jnp.dot(as_bf16(mine), before, preferred_element_type=F32)
    rank = jnp.sum(jnp.where(mine, ahead, 0.0), axis=0, keepdims=True).astype(I32)
    fits = live & (rank < CAP)
    spare = live & (rank >= CAP)
    spare_rank = jnp.dot(as_bf16(spare), before, preferred_element_type=F32).astype(I32)
    packed = spare & (spare_rank < SPARE)
    over = jnp.max(jnp.where(spare, spare_rank, 0), axis=1, keepdims=True) >= SPARE
    slot = jnp.where(fits, owner * MSG + rank, jnp.where(packed, SCEN * MSG + spare_rank, -1))
    gather = as_bf16(lax.broadcasted_iota(I32, (SCEN * MSG + PACK, ROWS), 0) == slot)

    def along_lanes(values, places):
        return lax.dot_general(
            values.astype(F32).astype(BF16), as_bf16(sublane == places), (((1,), (1,)), ((), ())), preferred_element_type=F32
        )

    keys = along_lanes(jnp.where(mine & fits, target + 1, 0), rank + s % 8 * MSG)

    def pack_keys(taken, device, place, lanes, spoilt, number):
        one = along_lanes(jnp.where(taken, device + 1, 0), lanes)
        two = along_lanes(jnp.where(taken, place, 0), lanes)
        return jnp.where(lane == number * PACK + SPARE, jnp.where(spoilt, -1.0, 0.0), one * 256.0 + two)

    spare_keys = pack_keys(packed, owner, target, spare_rank + i * PACK, over, i)

    row16 = lax.broadcasted_iota(I32, (16, 256), 0)
    lane256 = lax.broadcasted_iota(I32, (16, 256), 1)
    inv_col = jnp.max(jnp.where(ownv[...] == i * KC + row16, lane256 // KC, 0), axis=1, keepdims=True)
    inv_v[...] = jnp.broadcast_to(inv_col, (16, 128))
    inverse = pltpu.make_async_copy(inv_v, inv_s, small_sem.at[7])
    inverse.start()

    sub = lax.broadcasted_iota(I32, (8, BLK), 0)
    for t in range(ROWS // 8):
        if t in {0: 0, 8: 1}:
            loads[{0: 0, 8: 1}[t]].wait()
        w = weighted[8 * t : 8 * t + 8]
        lhs = jnp.concatenate([jnp.where(sub == g, w, 0.0) for g in range(8)], axis=1).astype(BF16)
        rhs = blk[8 * t : 8 * t + 8].reshape(8 * BLK, BLK)
        prod[pl.ds(8 * t, 8), :] = jnp.dot(lhs, rhs, preferred_element_type=F32)

    def exact(onehot, values):
        high = values.astype(BF16)
        low = (values - high.astype(F32)).astype(BF16)
        return jnp.dot(onehot, high, preferred_element_type=F32) + jnp.dot(onehot, low, preferred_element_type=F32)

    sent = exact(gather, prod[...])
    last = lax.broadcasted_iota(I32, (MSG, BLK), 0) == CAP
    for d in range(SCEN):
        msgs[d] = jnp.where(last, keys[d : d + 1], sent[d * MSG : (d + 1) * MSG])
    pack1[...] = jnp.where(sub == SPARE, spare_keys, sent[SCEN * MSG :])

    inverse.wait()
    pl.semaphore_wait(barrier, len(RING) + len(TORUS))

    def message(k, d, src):
        return pltpu.make_async_remote_copy(
            src_ref=msgs.at[d], dst_ref=landed.at[src],
            send_sem=msg_send.at[k], recv_sem=msg_recv.at[src],
            device_id=(d, i), device_id_type=MESH,
        )

    def first(k, e, src):
        return pltpu.make_async_remote_copy(
            src_ref=pack1, dst_ref=spare1.at[src], send_sem=first_send.at[k], recv_sem=first_recv.at[src],
            device_id=(s, e), device_id_type=MESH,
        )

    def second(k, d, src):
        return pltpu.make_async_remote_copy(
            src_ref=pack2, dst_ref=spare2.at[src], send_sem=second_send.at[k], recv_sem=second_recv.at[src],
            device_id=(d, i), device_id_type=MESH,
        )

    for k in range(15):
        message(k, scen_peers[k], s).start()
        first(k, clus_peers[k], i).start()
    pltpu.make_async_copy(msgs.at[s], landed.at[s], msg_recv.at[s]).start()
    pltpu.make_async_copy(pack1, spare1.at[i], first_recv.at[i]).start()

    def read_keys(spares):
        key = spares[0, pl.ds(SPARE, 1), :]
        for n in range(1, 16):
            key = key + spares[n, pl.ds(SPARE, 1), :]
        whole = key.astype(I32)
        return key > 0.0, whole // 256 - 1, whole % 256, jnp.min(key, axis=1, keepdims=True) < 0.0

    for src in range(CLUS):
        first(0, i, src).wait_recv()
    valid, device, place, spoilt = read_keys(spare1)
    cut = place // OWN
    counted = jnp.sum(
        jnp.where(valid & (lax.broadcasted_iota(I32, (CLUS, ROWS), 0) == cut), 1.0, 0.0), axis=1, keepdims=True
    )
    spoilt = spoilt | (jnp.max(counted, axis=0, keepdims=True) > SPARE)
    hit = valid & (cut == i)
    hit_rank = jnp.dot(as_bf16(hit), before, preferred_element_type=F32).astype(I32)
    hit = hit & (hit_rank < SPARE)
    second_keys = pack_keys(hit, device, lane // PACK * OWN + place % OWN, hit_rank + s * PACK, spoilt, s)
    moved = exact(as_bf16((sub == hit_rank) & hit), spare1[...].reshape(ROWS, BLK))
    pack2[...] = jnp.where(sub == SPARE, second_keys, moved)
    for k, p in enumerate(scen_peers):
        second(k, p, s).start()
    pltpu.make_async_copy(pack2, spare2.at[s], second_recv.at[s]).start()

    cell = lax.broadcasted_iota(I32, (CLUS * OWN, ROWS), 0)
    for step in range(2):
        group = (z // 4 + step) % 2 * 8
        for a in range(8):
            message(0, s, group + a).wait_recv()
        key = landed[group, pl.ds(CAP, 1), :]
        for a in range(1, 8):
            key = key + landed[group + a, pl.ds(CAP, 1), :]
        part = exact(as_bf16(cell == key.astype(I32) - 1), landed[pl.ds(group, 8)].reshape(8 * MSG, BLK))
        total[...] = part if step == 0 else total[...] + part

    def row(k, e, src):
        return pltpu.make_async_remote_copy(
            src_ref=total.at[pl.ds(e * OWN, OWN), :], dst_ref=rows.at[src],
            send_sem=row_send.at[k], recv_sem=row_recv.at[src],
            device_id=(s, e), device_id_type=MESH,
        )

    for k, p in enumerate(clus_peers):
        row(k, p, i).start()
    pltpu.make_async_copy(total.at[pl.ds(i * OWN, OWN), :], rows.at[i], row_recv.at[i]).start()
    for src in range(CLUS):
        row(0, i, src).wait_recv()
    for src in range(SCEN):
        second(0, s, src).wait_recv()
    valid, device, place, spoilt = read_keys(spare2)
    here = as_bf16(cell == jnp.where(valid & (device == s), place, -1))
    late[...] = exact(here, spare2[...].reshape(ROWS, BLK)).reshape(CLUS, OWN, BLK)
    flag[0, 0] = jnp.max(jnp.where(spoilt, 1, 0))
    for r in range(KC):
        line = rows[inv_s[r, 0]] + late[inv_s[r, 0]]
        for cb in range(OWN):
            out[pl.ds(r, 1), pl.ds(cb * BLK, BLK)] = line[cb : cb + 1]
    for k in range(15):
        message(k, scen_peers[k], s).wait_send()
        second(k, scen_peers[k], s).wait_send()
        first(k, clus_peers[k], i).wait_send()
        row(k, clus_peers[k], i).wait_send()


def body(duals, blocks, prob, cluster_map, block_cols, counts, cut_owner_rows):
    dma = pltpu.SemaphoreType.DMA
    arrays = (
        duals.reshape(ROWS, BLK),
        blocks.reshape(ROWS, BLK, BLK),
        prob.reshape(1, 64),
        cluster_map.reshape(1, 64),
        block_cols.T,
        counts.reshape(1, 1),
        cut_owner_rows,
        cut_owner_rows.reshape(1, 256),
    )
    inputs = [
        pltpu.VMEM((ROWS, BLK, BLK), BF16),
        pltpu.VMEM((ROWS, BLK), BF16),
        pltpu.VMEM((1, 64), F32),
        pltpu.VMEM((1, 64), I32),
        pltpu.VMEM((2, 64), I32),
        pltpu.SMEM((1, 1), I32),
        pltpu.SMEM((256,), I32),
        pltpu.VMEM((1, 256), I32),
        pltpu.VMEM((16, 128), I32),
        pltpu.SMEM((16, 128), I32),
    ]
    block = pltpu.VMEM((KC, OWN * BLK), F32)
    vmem = pl.BlockSpec(memory_space=pltpu.VMEM)

    def call(fn, shapes, specs, scratch, cid):
        return pl.pallas_call(
            fn,
            out_shape=shapes,
            in_specs=[pl.BlockSpec(memory_space=pltpu.HBM)] * len(arrays),
            out_specs=specs,
            scratch_shapes=inputs + scratch,
            compiler_params=pltpu.CompilerParams(
                collective_id=cid, has_side_effects=True, vmem_limit_bytes=60 << 20
            ),
        )(*arrays)

    def gathered():
        scratch = [
            pltpu.VMEM((SCEN, PIECE, BLK), F32),
            pltpu.VMEM((CLUS * OWN, BLK), F32),
            pltpu.VMEM((CLUS, OWN, BLK), F32),
            dma((8,)),
            dma((4,)),
            dma((2, 4, 4)),
            dma((2, 4, 4)),
            dma((2, 5, 4)),
            dma((2, 5, 4)),
            dma((CLUS,)),
            dma((CLUS,)),
        ]
        return call(kernel, block, vmem, scratch, 0)

    scratch = [
        pltpu.VMEM((ROWS, BLK), F32),
        pltpu.VMEM((SCEN, MSG, BLK), F32),
        pltpu.VMEM((SCEN, MSG, BLK), F32),
        pltpu.VMEM((CLUS * OWN, BLK), F32),
        pltpu.VMEM((CLUS, OWN, BLK), F32),
        pltpu.VMEM((PACK, BLK), F32),
        pltpu.VMEM((PACK, BLK), F32),
        pltpu.VMEM((CLUS, PACK, BLK), F32),
        pltpu.VMEM((SCEN, PACK, BLK), F32),
        pltpu.VMEM((CLUS, OWN, BLK), F32),
        dma((8,)),
        dma((4,)),
    ] + [dma((16,))] * 8
    flag = pltpu.SMEM((1, 1), I32)
    out, full = call(routed, (block, flag), (vmem, pl.BlockSpec(memory_space=pltpu.SMEM)), scratch, 1)
    return lax.switch(full[0, 0], (lambda: out, gathered))


def solution(mesh):
    placed = (
        P(("scen", "clus"), None, None),
        P(("scen", "clus"), None, None, None),
        P(("scen", "clus")),
        P(("scen", "clus")),
        P(("scen", "clus"), None),
        P(("scen", "clus")),
        P(),
    )
    return jax.shard_map(
        body, mesh=mesh, in_specs=placed, out_specs=P("clus", "scen"), check_vma=False
    )
```

```python
import functools

import jax
import jax.numpy as jnp
from jax import lax
from jax.experimental import pallas as pl
from jax.experimental.pallas import tpu as pltpu
from jax.sharding import PartitionSpec as P

N1 = 32768
KC = 16
BLK = 128
ROWS = 128
SCEN = 16
CLUS = 16
OWN = 16
PIECE = 136
CHUNKS = ((96, 40), (64, 32), (32, 32), (0, 32))
MESH = pl.DeviceIdType.MESH
F32, BF16, I32 = jnp.float32, jnp.bfloat16, jnp.int32


def travels(direction, hop, chunk):
    return hop <= 3 or (hop == 4 and (chunk < 2) == (direction == 0))


def kernel(
    duals_h, blocks_h, prob_h, cmap_h, cols_h, counts_h, owners_h, owners2_h, out,
    blk, dua, prb, cmp, col, cnt, own, ownv, inv_v, inv_s, pieces, total, landed,
    small_sem, blk_sem, ring_send, ring_recv, sib_send, sib_recv, row_send, row_recv,
):
    s, i = lax.axis_index("scen"), lax.axis_index("clus")
    right, left, sibling = (s + 2) % SCEN, (s + SCEN - 2) % SCEN, s + 1 - 2 * (s % 2)
    nc = len(CHUNKS)

    smalls = [
        pltpu.make_async_copy(src, dst, small_sem.at[n])
        for n, (src, dst) in enumerate(
            ((counts_h, cnt), (owners_h, own), (prob_h, prb), (duals_h, dua), (cmap_h, cmp), (cols_h, col), (owners2_h, ownv))
        )
    ]
    for c in smalls:
        c.start()
    loads = []
    for n, (lo, rows) in enumerate(CHUNKS):
        c = pltpu.make_async_copy(blocks_h.at[pl.ds(lo, 32)], blk.at[pl.ds(lo, 32)], blk_sem.at[n])
        c.start()
        loads.append(c)

    barrier = pltpu.get_barrier_semaphore()
    for dev in (right, left, sibling):
        pl.semaphore_signal(barrier, inc=1, device_id=(dev, i), device_id_type=MESH)
    for k in range(1, CLUS):
        pl.semaphore_signal(barrier, inc=1, device_id=(s, (i + k) % CLUS), device_id_type=MESH)

    for c in smalls:
        c.wait()

    lane64 = lax.broadcasted_iota(I32, (1, 64), 1)
    weight = jnp.where(lane64 < cnt[0, 0], prb[...], 0.0)
    spread = (lax.broadcasted_iota(I32, (ROWS, 64), 0) // 2) == lax.broadcasted_iota(I32, (ROWS, 64), 1)
    weight_col = jnp.sum(jnp.where(spread, weight, 0.0), axis=1, keepdims=True)
    weighted = (weight_col * dua[...].astype(F32)).astype(BF16).astype(F32)

    pick = (
        lax.broadcasted_iota(I32, (64, ROWS), 0) == lax.broadcasted_iota(I32, (64, ROWS), 1) // 2
    ).astype(F32).astype(BF16)
    both = jnp.dot(col[...].astype(F32).astype(BF16), pick, preferred_element_type=F32)
    cluster = jnp.dot(cmp[...].astype(F32).astype(BF16), pick, preferred_element_type=F32)
    lane = lax.broadcasted_iota(I32, (1, ROWS), 1)
    column = jnp.where(lane % 2 == 0, both[0:1], both[1:2])
    dest = jnp.zeros((1, ROWS), I32)
    cluster = cluster.astype(I32)
    for c in range(KC):
        dest = jnp.where(cluster == c, own[i * KC + c] // KC, dest)
    keys = dest.astype(F32) * 256.0 + column
    pieces[s, pl.ds(ROWS, 8), :] = jnp.broadcast_to(keys, (8, ROWS))

    def ring_copy(direction, hop, n):
        lo, rows = CHUNKS[n]
        source = (s + (SCEN - 2 * (hop - 1) if direction == 0 else 2 * (hop - 1))) % SCEN
        ref = pieces.at[source, pl.ds(lo, rows), :]
        return pltpu.make_async_remote_copy(
            src_ref=ref, dst_ref=ref,
            send_sem=ring_send.at[direction, hop - 1, n], recv_sem=ring_recv.at[direction, hop - 1, n],
            device_id=(right if direction == 0 else left, i), device_id_type=MESH,
        )

    def sib_copy(direction, hop, n):
        lo, rows = CHUNKS[n]
        source = (s + (SCEN - 2 * hop if direction == 0 else 2 * hop)) % SCEN
        ref = pieces.at[source, pl.ds(lo, rows), :]
        return pltpu.make_async_remote_copy(
            src_ref=ref, dst_ref=ref,
            send_sem=sib_send.at[direction, hop, n], recv_sem=sib_recv.at[direction, hop, n],
            device_id=(sibling, i), device_id_type=MESH,
        )

    started = []

    def start(copy):
        copy.start()
        started.append(copy)

    sub = lax.broadcasted_iota(I32, (8, BLK), 0)
    for n, (lo, rows) in enumerate(CHUNKS):
        loads[n].wait()
        for t in range(4):
            at = lo + 8 * t
            w = weighted[at : at + 8]
            lhs = jnp.concatenate([jnp.where(sub == g, w, 0.0) for g in range(8)], axis=1).astype(BF16)
            rhs = blk[at : at + 8].reshape(8 * BLK, BLK)
            pieces[s, pl.ds(at, 8), :] = jnp.dot(lhs, rhs, preferred_element_type=F32)
        if n == 0:
            pl.semaphore_wait(barrier, 3 + CLUS - 1)
        start(ring_copy(0, 1, n))
        start(ring_copy(1, 1, n))
        start(sib_copy(0, 0, n))

    total[...] = jnp.zeros_like(total)
    target = lax.broadcasted_iota(I32, (CLUS * OWN, ROWS), 0)

    def hot(source):
        key = pieces[source, pl.ds(ROWS, 1), :].astype(I32)
        cb = key % 256 - s * OWN
        t = jnp.where((cb >= 0) & (cb < OWN), key // 256 * OWN + cb, -1)
        return (target == t).astype(F32).astype(BF16)

    def add(first, second):
        onehot = jnp.concatenate([hot(first), hot(second)], axis=1)
        p = jnp.concatenate([pieces[first, pl.ds(0, ROWS), :], pieces[second, pl.ds(0, ROWS), :]], axis=0)
        high = p.astype(BF16)
        low = (p - high.astype(F32)).astype(BF16)
        total[...] += jnp.dot(onehot, high, preferred_element_type=F32) + jnp.dot(
            onehot, low, preferred_element_type=F32
        )

    def place(direction, hop, of=None):
        of = s if of is None else of
        return (of + (SCEN - 2 * hop if direction == 0 else 2 * hop)) % SCEN

    def add_hop(direction, hop):
        for n in range(nc):
            sib_copy(direction, hop, n).wait_recv()
        add(place(direction, hop), place(direction, hop, sibling))

    lane256 = lax.broadcasted_iota(I32, (16, 256), 1)
    row16 = lax.broadcasted_iota(I32, (16, 256), 0)
    ownrow = ownv[...]
    inv_col = jnp.max(jnp.where(ownrow == i * KC + row16, lane256 // KC, 0), axis=1, keepdims=True)
    inv_v[...] = jnp.broadcast_to(inv_col, (16, 128))
    c = pltpu.make_async_copy(inv_v, inv_s, small_sem.at[0])
    c.start()
    c.wait()

    for hop in range(1, 5):
        for n in range(nc):
            for direction in (0, 1):
                if travels(direction, hop, n):
                    ring_copy(direction, hop, n).wait_recv()
                    if travels(direction, hop + 1, n):
                        start(ring_copy(direction, hop + 1, n))
                    start(sib_copy(direction, hop, n))
            if n == 1:
                if hop == 1:
                    add_hop(0, 0)
                else:
                    add_hop(0, hop - 1)
            if n == 3 and hop > 1:
                add_hop(1, hop - 1)
    for n in range(nc):
        sib_copy(0 if n < 2 else 1, 4, n).wait_recv()
    add(place(0, 4), place(0, 4, sibling))

    rows_out = []
    for k in range(1, CLUS):
        e = (i + k) % CLUS
        c = pltpu.make_async_remote_copy(
            src_ref=total.at[pl.ds(e * OWN, OWN), :], dst_ref=landed.at[i],
            send_sem=row_send.at[k], recv_sem=row_recv.at[k],
            device_id=(s, e), device_id_type=MESH,
        )
        c.start()
        rows_out.append(c)
    landed[i] = total[pl.ds(i * OWN, OWN), :]
    for c in rows_out:
        c.wait_recv()
    for r in range(KC):
        row = landed[inv_s[r, 0]]
        for cb in range(OWN):
            out[pl.ds(r, 1), pl.ds(cb * BLK, BLK)] = row[cb : cb + 1]
    for c in rows_out:
        c.wait_send()
    for c in started:
        c.wait_send()


CAP = 15
MSG = 16
SPARE = 7
PACK = 8
RING = tuple((dz, dc) for dz in (4, 3, 5, 2, 6, 1, 7, 0) for dc in (0, 1) if (dz, dc) != (0, 0))
TORUS = tuple(
    sorted(
        ((dy, dx) for dy in range(4) for dx in range(4) if (dy, dx) != (0, 0)),
        key=lambda d: -(min(d[0], 4 - d[0]) + min(d[1], 4 - d[1])),
    )
)


def routed(
    duals_h, blocks_h, prob_h, cmap_h, cols_h, counts_h, owners_h, owners2_h, out, flag,
    blk, dua, prb, cmp, col, cnt, own, ownv, inv_v, inv_s, prod, msgs, landed, total, rows,
    pack1, pack2, spare1, spare2, late,
    small_sem, blk_sem, msg_send, msg_recv, row_send, row_recv, first_send, first_recv, second_send, second_recv,
):
    s, i = lax.axis_index("scen"), lax.axis_index("clus")
    z, c, y, x = s // 2, s % 2, i // 4, i % 4
    scen_peers = [(z + dz) % 8 * 2 + (c if dc == 0 else 1 - c) for dz, dc in RING]
    clus_peers = [(y + dy) % 4 * 4 + (x + dx) % 4 for dy, dx in TORUS]

    smalls = [
        pltpu.make_async_copy(src, dst, small_sem.at[n])
        for n, (src, dst) in enumerate(
            ((counts_h, cnt), (owners_h, own), (prob_h, prb), (duals_h, dua), (cmap_h, cmp), (cols_h, col), (owners2_h, ownv))
        )
    ]
    for copy in smalls:
        copy.start()
    loads = []
    for n, (at, many) in enumerate(((0, 64), (64, 64))):
        part = pl.ds(at, many)
        loads.append(pltpu.make_async_copy(blocks_h.at[part], blk.at[part], blk_sem.at[n]))
        loads[-1].start()


    barrier = pltpu.get_barrier_semaphore()
    for p in scen_peers:
        pl.semaphore_signal(barrier, inc=1, device_id=(p, i), device_id_type=MESH)

    for p in clus_peers:
        pl.semaphore_signal(barrier, inc=1, device_id=(s, p), device_id_type=MESH)

    for copy in smalls:
        copy.wait()

    lane64 = lax.broadcasted_iota(I32, (1, 64), 1)
    weight = jnp.where(lane64 < cnt[0, 0], prb[...], 0.0)
    spread = (lax.broadcasted_iota(I32, (ROWS, 64), 0) // 2) == lax.broadcasted_iota(I32, (ROWS, 64), 1)
    weight_col = jnp.sum(jnp.where(spread, weight, 0.0), axis=1, keepdims=True)
    weighted = (weight_col * dua[...].astype(F32)).astype(BF16).astype(F32)

    def as_bf16(mask):
        return mask.astype(F32).astype(BF16)

    pick = as_bf16(lax.broadcasted_iota(I32, (64, ROWS), 0) == lax.broadcasted_iota(I32, (64, ROWS), 1) // 2)
    both = jnp.dot(col[...].astype(F32).astype(BF16), pick, preferred_element_type=F32)
    cluster = jnp.dot(cmp[...].astype(F32).astype(BF16), pick, preferred_element_type=F32).astype(I32)
    lane = lax.broadcasted_iota(I32, (1, ROWS), 1)
    column = jnp.where(lane % 2 == 0, both[0:1], both[1:2]).astype(I32)
    live = lane // 2 < cnt[0, 0]
    dest = jnp.zeros((1, ROWS), I32)
    for k in range(KC):
        dest = jnp.where(cluster == k, own[i * KC + k] // KC, dest)
    owner = jnp.where(live, column // OWN, -1)
    target = dest * OWN + column % OWN
    mine = lax.broadcasted_iota(I32, (SCEN, ROWS), 0) == owner
    sublane = lax.broadcasted_iota(I32, (ROWS, ROWS), 0)
    before = as_bf16(sublane < lax.broadcasted_iota(I32, (ROWS, ROWS), 1))
    ahead = jnp.dot(as_bf16(mine), before, preferred_element_type=F32)
    rank = jnp.sum(jnp.where(mine, ahead, 0.0), axis=0, keepdims=True).astype(I32)
    fits = live & (rank < CAP)
    spare = live & (rank >= CAP)
    spare_rank = jnp.dot(as_bf16(spare), before, preferred_element_type=F32).astype(I32)
    packed = spare & (spare_rank < SPARE)
    over = jnp.max(jnp.where(spare, spare_rank, 0), axis=1, keepdims=True) >= SPARE
    slot = jnp.where(fits, owner * MSG + rank, jnp.where(packed, SCEN * MSG + spare_rank, -1))
    gather = as_bf16(lax.broadcasted_iota(I32, (SCEN * MSG + PACK, ROWS), 0) == slot)

    def along_lanes(values, places):
        return lax.dot_general(
            values.astype(F32).astype(BF16), as_bf16(sublane == places), (((1,), (1,)), ((), ())), preferred_element_type=F32
        )

    keys = along_lanes(jnp.where(mine & fits, target + 1, 0), rank + s % 8 * MSG)

    def pack_keys(taken, device, place, lanes, spoilt, number):
        one = along_lanes(jnp.where(taken, device + 1, 0), lanes)
        two = along_lanes(jnp.where(taken, place, 0), lanes)
        return jnp.where(lane == number * PACK + SPARE, jnp.where(spoilt, -1.0, 0.0), one * 256.0 + two)

    spare_keys = pack_keys(packed, owner, target, spare_rank + i * PACK, over, i)

    sub = lax.broadcasted_iota(I32, (8, BLK), 0)
    for t in range(ROWS // 8):
        if t in {0: 0, 8: 1}:
            loads[{0: 0, 8: 1}[t]].wait()
        w = weighted[8 * t : 8 * t + 8]
        lhs = jnp.concatenate([jnp.where(sub == g, w, 0.0) for g in range(8)], axis=1).astype(BF16)
        rhs = blk[8 * t : 8 * t + 8].reshape(8 * BLK, BLK)
        prod[pl.ds(8 * t, 8), :] = jnp.dot(lhs, rhs, preferred_element_type=F32)

    def exact(onehot, values):
        high = values.astype(BF16)
        low = (values - high.astype(F32)).astype(BF16)
        return jnp.dot(onehot, high, preferred_element_type=F32) + jnp.dot(onehot, low, preferred_element_type=F32)

    sent = exact(gather, prod[...])
    last = lax.broadcasted_iota(I32, (MSG, BLK), 0) == CAP
    for d in range(SCEN):
        msgs[d] = jnp.where(last, keys[d : d + 1], sent[d * MSG : (d + 1) * MSG])
    pack1[...] = jnp.where(sub == SPARE, spare_keys, sent[SCEN * MSG :])

    pl.semaphore_wait(barrier, len(RING) + len(TORUS))

    def message(k, d, src):
        return pltpu.make_async_remote_copy(
            src_ref=msgs.at[d], dst_ref=landed.at[src],
            send_sem=msg_send.at[k], recv_sem=msg_recv.at[src],
            device_id=(d, i), device_id_type=MESH,
        )

    def first(k, e, src):
        return pltpu.make_async_remote_copy(
            src_ref=pack1, dst_ref=spare1.at[src], send_sem=first_send.at[k], recv_sem=first_recv.at[src],
            device_id=(s, e), device_id_type=MESH,
        )

    def second(k, d, src):
        return pltpu.make_async_remote_copy(
            src_ref=pack2, dst_ref=spare2.at[src], send_sem=second_send.at[k], recv_sem=second_recv.at[src],
            device_id=(d, i), device_id_type=MESH,
        )

    for k in range(15):
        first(k, clus_peers[k], i).start()
    for k in range(15):
        message(k, scen_peers[k], s).start()
    pltpu.make_async_copy(msgs.at[s], landed.at[s], msg_recv.at[s]).start()
    pltpu.make_async_copy(pack1, spare1.at[i], first_recv.at[i]).start()

    row16 = lax.broadcasted_iota(I32, (16, 256), 0)
    lane256 = lax.broadcasted_iota(I32, (16, 256), 1)
    inv_col = jnp.max(jnp.where(ownv[...] == i * KC + row16, lane256 // KC, 0), axis=1, keepdims=True)
    inv_v[...] = jnp.broadcast_to(inv_col, (16, 128))
    inverse = pltpu.make_async_copy(inv_v, inv_s, small_sem.at[7])
    inverse.start()

    def read_keys(spares):
        key = spares[0, pl.ds(SPARE, 1), :]
        for n in range(1, 16):
            key = key + spares[n, pl.ds(SPARE, 1), :]
        whole = key.astype(I32)
        return key > 0.0, whole // 256 - 1, whole % 256, jnp.min(key, axis=1, keepdims=True) < 0.0

    for src in range(CLUS):
        first(0, i, src).wait_recv()
    valid, device, place, spoilt = read_keys(spare1)
    cut = place // OWN
    counted = jnp.sum(
        jnp.where(valid & (lax.broadcasted_iota(I32, (CLUS, ROWS), 0) == cut), 1.0, 0.0), axis=1, keepdims=True
    )
    spoilt = spoilt | (jnp.max(counted, axis=0, keepdims=True) > SPARE)
    hit = valid & (cut == i)
    hit_rank = jnp.dot(as_bf16(hit), before, preferred_element_type=F32).astype(I32)
    hit = hit & (hit_rank < SPARE)
    second_keys = pack_keys(hit, device, lane // PACK * OWN + place % OWN, hit_rank + s * PACK, spoilt, s)
    moved = exact(as_bf16((sub == hit_rank) & hit), spare1[...].reshape(ROWS, BLK))
    pack2[...] = jnp.where(sub == SPARE, second_keys, moved)
    for k, p in enumerate(scen_peers):
        second(k, p, s).start()
    pltpu.make_async_copy(pack2, spare2.at[s], second_recv.at[s]).start()

    cell = lax.broadcasted_iota(I32, (CLUS * OWN, ROWS), 0)
    for step in range(2):
        group = (z // 4 + step) % 2 * 8
        for a in range(8):
            message(0, s, group + a).wait_recv()
        key = landed[group, pl.ds(CAP, 1), :]
        for a in range(1, 8):
            key = key + landed[group + a, pl.ds(CAP, 1), :]
        part = exact(as_bf16(cell == key.astype(I32) - 1), landed[pl.ds(group, 8)].reshape(8 * MSG, BLK))
        total[...] = part if step == 0 else total[...] + part

    def row(k, e, src):
        return pltpu.make_async_remote_copy(
            src_ref=total.at[pl.ds(e * OWN, OWN), :], dst_ref=rows.at[src],
            send_sem=row_send.at[k], recv_sem=row_recv.at[src],
            device_id=(s, e), device_id_type=MESH,
        )

    for k, p in enumerate(clus_peers):
        row(k, p, i).start()
    pltpu.make_async_copy(total.at[pl.ds(i * OWN, OWN), :], rows.at[i], row_recv.at[i]).start()
    inverse.wait()
    for src in range(SCEN):
        second(0, s, src).wait_recv()
    valid, device, place, spoilt = read_keys(spare2)
    here = as_bf16(cell == jnp.where(valid & (device == s), place, -1))
    late[...] = exact(here, spare2[...].reshape(ROWS, BLK)).reshape(CLUS, OWN, BLK)
    flag[0, 0] = jnp.max(jnp.where(spoilt, 1, 0))
    for src in range(CLUS):
        row(0, i, src).wait_recv()
    for r in range(KC):
        line = rows[inv_s[r, 0]] + late[inv_s[r, 0]]
        for cb in range(OWN):
            out[pl.ds(r, 1), pl.ds(cb * BLK, BLK)] = line[cb : cb + 1]
    for k in range(15):
        message(k, scen_peers[k], s).wait_send()
        second(k, scen_peers[k], s).wait_send()
        first(k, clus_peers[k], i).wait_send()
        row(k, clus_peers[k], i).wait_send()


def body(duals, blocks, prob, cluster_map, block_cols, counts, cut_owner_rows):
    dma = pltpu.SemaphoreType.DMA
    arrays = (
        duals.reshape(ROWS, BLK),
        blocks.reshape(ROWS, BLK, BLK),
        prob.reshape(1, 64),
        cluster_map.reshape(1, 64),
        block_cols.T,
        counts.reshape(1, 1),
        cut_owner_rows,
        cut_owner_rows.reshape(1, 256),
    )
    inputs = [
        pltpu.VMEM((ROWS, BLK, BLK), BF16),
        pltpu.VMEM((ROWS, BLK), BF16),
        pltpu.VMEM((1, 64), F32),
        pltpu.VMEM((1, 64), I32),
        pltpu.VMEM((2, 64), I32),
        pltpu.SMEM((1, 1), I32),
        pltpu.SMEM((256,), I32),
        pltpu.VMEM((1, 256), I32),
        pltpu.VMEM((16, 128), I32),
        pltpu.SMEM((16, 128), I32),
    ]
    block = pltpu.VMEM((KC, OWN * BLK), F32)
    vmem = pl.BlockSpec(memory_space=pltpu.VMEM)

    def call(fn, shapes, specs, scratch, cid):
        return pl.pallas_call(
            fn,
            out_shape=shapes,
            in_specs=[pl.BlockSpec(memory_space=pltpu.HBM)] * len(arrays),
            out_specs=specs,
            scratch_shapes=inputs + scratch,
            compiler_params=pltpu.CompilerParams(
                collective_id=cid, has_side_effects=True, vmem_limit_bytes=60 << 20
            ),
        )(*arrays)

    def gathered():
        scratch = [
            pltpu.VMEM((SCEN, PIECE, BLK), F32),
            pltpu.VMEM((CLUS * OWN, BLK), F32),
            pltpu.VMEM((CLUS, OWN, BLK), F32),
            dma((8,)),
            dma((4,)),
            dma((2, 4, 4)),
            dma((2, 4, 4)),
            dma((2, 5, 4)),
            dma((2, 5, 4)),
            dma((CLUS,)),
            dma((CLUS,)),
        ]
        return call(kernel, block, vmem, scratch, 0)

    scratch = [
        pltpu.VMEM((ROWS, BLK), F32),
        pltpu.VMEM((SCEN, MSG, BLK), F32),
        pltpu.VMEM((SCEN, MSG, BLK), F32),
        pltpu.VMEM((CLUS * OWN, BLK), F32),
        pltpu.VMEM((CLUS, OWN, BLK), F32),
        pltpu.VMEM((PACK, BLK), F32),
        pltpu.VMEM((PACK, BLK), F32),
        pltpu.VMEM((CLUS, PACK, BLK), F32),
        pltpu.VMEM((SCEN, PACK, BLK), F32),
        pltpu.VMEM((CLUS, OWN, BLK), F32),
        dma((8,)),
        dma((4,)),
    ] + [dma((16,))] * 8
    flag = pltpu.SMEM((1, 1), I32)
    out, full = call(routed, (block, flag), (vmem, pl.BlockSpec(memory_space=pltpu.SMEM)), scratch, 1)
    return lax.switch(full[0, 0], (lambda: out, gathered))


def solution(mesh):
    placed = (
        P(("scen", "clus"), None, None),
        P(("scen", "clus"), None, None, None),
        P(("scen", "clus")),
        P(("scen", "clus")),
        P(("scen", "clus"), None),
        P(("scen", "clus")),
        P(),
    )
    return jax.shard_map(
        body, mesh=mesh, in_specs=placed, out_specs=P("clus", "scen"), check_vma=False
    )
```

```python
import functools

import jax
import jax.numpy as jnp
from jax import lax
from jax.experimental import pallas as pl
from jax.experimental.pallas import tpu as pltpu
from jax.sharding import PartitionSpec as P

N1 = 32768
KC = 16
BLK = 128
ROWS = 128
SCEN = 16
CLUS = 16
OWN = 16
PIECE = 136
CHUNKS = ((96, 40), (64, 32), (32, 32), (0, 32))
MESH = pl.DeviceIdType.MESH
F32, BF16, I32 = jnp.float32, jnp.bfloat16, jnp.int32


def travels(direction, hop, chunk):
    return hop <= 3 or (hop == 4 and (chunk < 2) == (direction == 0))


def kernel(
    duals_h, blocks_h, prob_h, cmap_h, cols_h, counts_h, owners_h, owners2_h, out,
    blk, dua, prb, cmp, col, cnt, own, ownv, inv_v, inv_s, pieces, total, landed,
    small_sem, blk_sem, ring_send, ring_recv, sib_send, sib_recv, row_send, row_recv,
):
    s, i = lax.axis_index("scen"), lax.axis_index("clus")
    right, left, sibling = (s + 2) % SCEN, (s + SCEN - 2) % SCEN, s + 1 - 2 * (s % 2)
    nc = len(CHUNKS)

    smalls = [
        pltpu.make_async_copy(src, dst, small_sem.at[n])
        for n, (src, dst) in enumerate(
            ((counts_h, cnt), (owners_h, own), (prob_h, prb), (duals_h, dua), (cmap_h, cmp), (cols_h, col), (owners2_h, ownv))
        )
    ]
    for c in smalls:
        c.start()
    loads = []
    for n, (lo, rows) in enumerate(CHUNKS):
        c = pltpu.make_async_copy(blocks_h.at[pl.ds(lo, 32)], blk.at[pl.ds(lo, 32)], blk_sem.at[n])
        c.start()
        loads.append(c)

    barrier = pltpu.get_barrier_semaphore()
    for dev in (right, left, sibling):
        pl.semaphore_signal(barrier, inc=1, device_id=(dev, i), device_id_type=MESH)
    for k in range(1, CLUS):
        pl.semaphore_signal(barrier, inc=1, device_id=(s, (i + k) % CLUS), device_id_type=MESH)

    for c in smalls:
        c.wait()

    lane64 = lax.broadcasted_iota(I32, (1, 64), 1)
    weight = jnp.where(lane64 < cnt[0, 0], prb[...], 0.0)
    spread = (lax.broadcasted_iota(I32, (ROWS, 64), 0) // 2) == lax.broadcasted_iota(I32, (ROWS, 64), 1)
    weight_col = jnp.sum(jnp.where(spread, weight, 0.0), axis=1, keepdims=True)
    weighted = (weight_col * dua[...].astype(F32)).astype(BF16).astype(F32)

    pick = (
        lax.broadcasted_iota(I32, (64, ROWS), 0) == lax.broadcasted_iota(I32, (64, ROWS), 1) // 2
    ).astype(F32).astype(BF16)
    both = jnp.dot(col[...].astype(F32).astype(BF16), pick, preferred_element_type=F32)
    cluster = jnp.dot(cmp[...].astype(F32).astype(BF16), pick, preferred_element_type=F32)
    lane = lax.broadcasted_iota(I32, (1, ROWS), 1)
    column = jnp.where(lane % 2 == 0, both[0:1], both[1:2])
    dest = jnp.zeros((1, ROWS), I32)
    cluster = cluster.astype(I32)
    for c in range(KC):
        dest = jnp.where(cluster == c, own[i * KC + c] // KC, dest)
    keys = dest.astype(F32) * 256.0 + column
    pieces[s, pl.ds(ROWS, 8), :] = jnp.broadcast_to(keys, (8, ROWS))

    def ring_copy(direction, hop, n):
        lo, rows = CHUNKS[n]
        source = (s + (SCEN - 2 * (hop - 1) if direction == 0 else 2 * (hop - 1))) % SCEN
        ref = pieces.at[source, pl.ds(lo, rows), :]
        return pltpu.make_async_remote_copy(
            src_ref=ref, dst_ref=ref,
            send_sem=ring_send.at[direction, hop - 1, n], recv_sem=ring_recv.at[direction, hop - 1, n],
            device_id=(right if direction == 0 else left, i), device_id_type=MESH,
        )

    def sib_copy(direction, hop, n):
        lo, rows = CHUNKS[n]
        source = (s + (SCEN - 2 * hop if direction == 0 else 2 * hop)) % SCEN
        ref = pieces.at[source, pl.ds(lo, rows), :]
        return pltpu.make_async_remote_copy(
            src_ref=ref, dst_ref=ref,
            send_sem=sib_send.at[direction, hop, n], recv_sem=sib_recv.at[direction, hop, n],
            device_id=(sibling, i), device_id_type=MESH,
        )

    started = []

    def start(copy):
        copy.start()
        started.append(copy)

    sub = lax.broadcasted_iota(I32, (8, BLK), 0)
    for n, (lo, rows) in enumerate(CHUNKS):
        loads[n].wait()
        for t in range(4):
            at = lo + 8 * t
            w = weighted[at : at + 8]
            lhs = jnp.concatenate([jnp.where(sub == g, w, 0.0) for g in range(8)], axis=1).astype(BF16)
            rhs = blk[at : at + 8].reshape(8 * BLK, BLK)
            pieces[s, pl.ds(at, 8), :] = jnp.dot(lhs, rhs, preferred_element_type=F32)
        if n == 0:
            pl.semaphore_wait(barrier, 3 + CLUS - 1)
        start(ring_copy(0, 1, n))
        start(ring_copy(1, 1, n))
        start(sib_copy(0, 0, n))

    total[...] = jnp.zeros_like(total)
    target = lax.broadcasted_iota(I32, (CLUS * OWN, ROWS), 0)

    def hot(source):
        key = pieces[source, pl.ds(ROWS, 1), :].astype(I32)
        cb = key % 256 - s * OWN
        t = jnp.where((cb >= 0) & (cb < OWN), key // 256 * OWN + cb, -1)
        return (target == t).astype(F32).astype(BF16)

    def add(first, second):
        onehot = jnp.concatenate([hot(first), hot(second)], axis=1)
        p = jnp.concatenate([pieces[first, pl.ds(0, ROWS), :], pieces[second, pl.ds(0, ROWS), :]], axis=0)
        high = p.astype(BF16)
        low = (p - high.astype(F32)).astype(BF16)
        total[...] += jnp.dot(onehot, high, preferred_element_type=F32) + jnp.dot(
            onehot, low, preferred_element_type=F32
        )

    def place(direction, hop, of=None):
        of = s if of is None else of
        return (of + (SCEN - 2 * hop if direction == 0 else 2 * hop)) % SCEN

    def add_hop(direction, hop):
        for n in range(nc):
            sib_copy(direction, hop, n).wait_recv()
        add(place(direction, hop), place(direction, hop, sibling))

    lane256 = lax.broadcasted_iota(I32, (16, 256), 1)
    row16 = lax.broadcasted_iota(I32, (16, 256), 0)
    ownrow = ownv[...]
    inv_col = jnp.max(jnp.where(ownrow == i * KC + row16, lane256 // KC, 0), axis=1, keepdims=True)
    inv_v[...] = jnp.broadcast_to(inv_col, (16, 128))
    c = pltpu.make_async_copy(inv_v, inv_s, small_sem.at[0])
    c.start()
    c.wait()

    for hop in range(1, 5):
        for n in range(nc):
            for direction in (0, 1):
                if travels(direction, hop, n):
                    ring_copy(direction, hop, n).wait_recv()
                    if travels(direction, hop + 1, n):
                        start(ring_copy(direction, hop + 1, n))
                    start(sib_copy(direction, hop, n))
            if n == 1:
                if hop == 1:
                    add_hop(0, 0)
                else:
                    add_hop(0, hop - 1)
            if n == 3 and hop > 1:
                add_hop(1, hop - 1)
    for n in range(nc):
        sib_copy(0 if n < 2 else 1, 4, n).wait_recv()
    add(place(0, 4), place(0, 4, sibling))

    rows_out = []
    for k in range(1, CLUS):
        e = (i + k) % CLUS
        c = pltpu.make_async_remote_copy(
            src_ref=total.at[pl.ds(e * OWN, OWN), :], dst_ref=landed.at[i],
            send_sem=row_send.at[k], recv_sem=row_recv.at[k],
            device_id=(s, e), device_id_type=MESH,
        )
        c.start()
        rows_out.append(c)
    landed[i] = total[pl.ds(i * OWN, OWN), :]
    for c in rows_out:
        c.wait_recv()
    for r in range(KC):
        row = landed[inv_s[r, 0]]
        for cb in range(OWN):
            out[pl.ds(r, 1), pl.ds(cb * BLK, BLK)] = row[cb : cb + 1]
    for c in rows_out:
        c.wait_send()
    for c in started:
        c.wait_send()


CAP = 15
MSG = 16
SPARE = 7
PACK = 8
RING = tuple((dz, dc) for dz in (4, 3, 5, 2, 6, 1, 7, 0) for dc in (0, 1) if (dz, dc) != (0, 0))
TORUS = tuple(
    sorted(
        ((dy, dx) for dy in range(4) for dx in range(4) if (dy, dx) != (0, 0)),
        key=lambda d: -(min(d[0], 4 - d[0]) + min(d[1], 4 - d[1])),
    )
)


def routed(
    duals_h, blocks_h, prob_h, cmap_h, cols_h, counts_h, owners_h, owners2_h, out, flag,
    blk, dua, prb, cmp, col, cnt, own, ownv, inv_v, inv_s, prod, msgs, landed, total, rows,
    pack1, pack2, spare1, spare2, late,
    small_sem, blk_sem, msg_send, msg_recv, row_send, row_recv, first_send, first_recv, second_send, second_recv,
):
    s, i = lax.axis_index("scen"), lax.axis_index("clus")
    z, c, y, x = s // 2, s % 2, i // 4, i % 4
    scen_peers = [(z + dz) % 8 * 2 + (c if dc == 0 else 1 - c) for dz, dc in RING]
    clus_peers = [(y + dy) % 4 * 4 + (x + dx) % 4 for dy, dx in TORUS]

    smalls = [
        pltpu.make_async_copy(src, dst, small_sem.at[n])
        for n, (src, dst) in enumerate(
            ((counts_h, cnt), (owners_h, own), (prob_h, prb), (duals_h, dua), (cmap_h, cmp), (cols_h, col), (owners2_h, ownv))
        )
    ]
    for copy in smalls:
        copy.start()
    loads = []
    for n, (at, many) in enumerate(((0, 64), (64, 64))):
        part = pl.ds(at, many)
        loads.append(pltpu.make_async_copy(blocks_h.at[part], blk.at[part], blk_sem.at[n]))
        loads[-1].start()


    barrier = pltpu.get_barrier_semaphore()
    for p in scen_peers:
        pl.semaphore_signal(barrier, inc=1, device_id=(p, i), device_id_type=MESH)

    for p in clus_peers:
        pl.semaphore_signal(barrier, inc=1, device_id=(s, p), device_id_type=MESH)

    for copy in smalls:
        copy.wait()

    lane64 = lax.broadcasted_iota(I32, (1, 64), 1)
    weight = jnp.where(lane64 < cnt[0, 0], prb[...], 0.0)
    spread = (lax.broadcasted_iota(I32, (ROWS, 64), 0) // 2) == lax.broadcasted_iota(I32, (ROWS, 64), 1)
    weight_col = jnp.sum(jnp.where(spread, weight, 0.0), axis=1, keepdims=True)
    weighted = (weight_col * dua[...].astype(F32)).astype(BF16).astype(F32)

    def as_bf16(mask):
        return mask.astype(F32).astype(BF16)

    pick = as_bf16(lax.broadcasted_iota(I32, (64, ROWS), 0) == lax.broadcasted_iota(I32, (64, ROWS), 1) // 2)
    both = jnp.dot(col[...].astype(F32).astype(BF16), pick, preferred_element_type=F32)
    cluster = jnp.dot(cmp[...].astype(F32).astype(BF16), pick, preferred_element_type=F32).astype(I32)
    lane = lax.broadcasted_iota(I32, (1, ROWS), 1)
    column = jnp.where(lane % 2 == 0, both[0:1], both[1:2]).astype(I32)
    live = lane // 2 < cnt[0, 0]
    dest = jnp.zeros((1, ROWS), I32)
    for k in range(KC):
        dest = jnp.where(cluster == k, own[i * KC + k] // KC, dest)
    owner = jnp.where(live, column // OWN, -1)
    target = dest * OWN + column % OWN
    mine = lax.broadcasted_iota(I32, (SCEN, ROWS), 0) == owner
    sublane = lax.broadcasted_iota(I32, (ROWS, ROWS), 0)
    before = as_bf16(sublane < lax.broadcasted_iota(I32, (ROWS, ROWS), 1))
    ahead = jnp.dot(as_bf16(mine), before, preferred_element_type=F32)
    rank = jnp.sum(jnp.where(mine, ahead, 0.0), axis=0, keepdims=True).astype(I32)
    fits = live & (rank < CAP)
    spare = live & (rank >= CAP)
    spare_rank = jnp.dot(as_bf16(spare), before, preferred_element_type=F32).astype(I32)
    packed = spare & (spare_rank < SPARE)
    over = jnp.max(jnp.where(spare, spare_rank, 0), axis=1, keepdims=True) >= SPARE
    slot = jnp.where(fits, owner * MSG + rank, jnp.where(packed, SCEN * MSG + spare_rank, -1))
    gather = as_bf16(lax.broadcasted_iota(I32, (SCEN * MSG + PACK, ROWS), 0) == slot)

    def along_lanes(values, places):
        return lax.dot_general(
            values.astype(F32).astype(BF16), as_bf16(sublane == places), (((1,), (1,)), ((), ())), preferred_element_type=F32
        )

    keys = along_lanes(jnp.where(mine & fits, target + 1, 0), rank + s % 8 * MSG)

    def pack_keys(taken, device, place, lanes, spoilt, number):
        one = along_lanes(jnp.where(taken, device + 1, 0), lanes)
        two = along_lanes(jnp.where(taken, place, 0), lanes)
        return jnp.where(lane == number * PACK + SPARE, jnp.where(spoilt, -1.0, 0.0), one * 256.0 + two)

    spare_keys = pack_keys(packed, owner, target, spare_rank + i * PACK, over, i)

    sub = lax.broadcasted_iota(I32, (8, BLK), 0)
    for t in range(ROWS // 8):
        if t in {0: 0, 8: 1}:
            loads[{0: 0, 8: 1}[t]].wait()
        w = weighted[8 * t : 8 * t + 8]
        lhs = jnp.concatenate([jnp.where(sub == g, w, 0.0) for g in range(8)], axis=1).astype(BF16)
        rhs = blk[8 * t : 8 * t + 8].reshape(8 * BLK, BLK)
        prod[pl.ds(8 * t, 8), :] = jnp.dot(lhs, rhs, preferred_element_type=F32)

    def exact(onehot, values):
        high = values.astype(BF16)
        low = (values - high.astype(F32)).astype(BF16)
        return jnp.dot(
            jnp.concatenate([onehot, onehot], axis=1),
            jnp.concatenate([high, low], axis=0),
            preferred_element_type=F32,
        )

    sent = exact(gather, prod[...])
    last = lax.broadcasted_iota(I32, (MSG, BLK), 0) == CAP
    for d in range(SCEN):
        msgs[d] = jnp.where(last, keys[d : d + 1], sent[d * MSG : (d + 1) * MSG])
    pack1[...] = jnp.where(sub == SPARE, spare_keys, sent[SCEN * MSG :])

    pl.semaphore_wait(barrier, len(RING) + len(TORUS))

    def message(k, d, src):
        return pltpu.make_async_remote_copy(
            src_ref=msgs.at[d], dst_ref=landed.at[src],
            send_sem=msg_send.at[k], recv_sem=msg_recv.at[src],
            device_id=(d, i), device_id_type=MESH,
        )

    def first(k, e, src):
        return pltpu.make_async_remote_copy(
            src_ref=pack1, dst_ref=spare1.at[src], send_sem=first_send.at[k], recv_sem=first_recv.at[src],
            device_id=(s, e), device_id_type=MESH,
        )

    def second(k, d, src):
        return pltpu.make_async_remote_copy(
            src_ref=pack2, dst_ref=spare2.at[src], send_sem=second_send.at[k], recv_sem=second_recv.at[src],
            device_id=(d, i), device_id_type=MESH,
        )

    for k in range(15):
        first(k, clus_peers[k], i).start()
    for k in range(15):
        message(k, scen_peers[k], s).start()
    pltpu.make_async_copy(msgs.at[s], landed.at[s], msg_recv.at[s]).start()
    pltpu.make_async_copy(pack1, spare1.at[i], first_recv.at[i]).start()

    row16 = lax.broadcasted_iota(I32, (16, 256), 0)
    lane256 = lax.broadcasted_iota(I32, (16, 256), 1)
    inv_col = jnp.max(jnp.where(ownv[...] == i * KC + row16, lane256 // KC, 0), axis=1, keepdims=True)
    inv_v[...] = jnp.broadcast_to(inv_col, (16, 128))
    inverse = pltpu.make_async_copy(inv_v, inv_s, small_sem.at[7])
    inverse.start()

    def read_keys(spares):
        key = spares[0, pl.ds(SPARE, 1), :]
        for n in range(1, 16):
            key = key + spares[n, pl.ds(SPARE, 1), :]
        whole = key.astype(I32)
        return key > 0.0, whole // 256 - 1, whole % 256, jnp.min(key, axis=1, keepdims=True) < 0.0

    for src in range(CLUS):
        first(0, i, src).wait_recv()
    valid, device, place, spoilt = read_keys(spare1)
    cut = place // OWN
    counted = jnp.sum(
        jnp.where(valid & (lax.broadcasted_iota(I32, (CLUS, ROWS), 0) == cut), 1.0, 0.0), axis=1, keepdims=True
    )
    spoilt = spoilt | (jnp.max(counted, axis=0, keepdims=True) > SPARE)
    hit = valid & (cut == i)
    hit_rank = jnp.dot(as_bf16(hit), before, preferred_element_type=F32).astype(I32)
    hit = hit & (hit_rank < SPARE)
    second_keys = pack_keys(hit, device, lane // PACK * OWN + place % OWN, hit_rank + s * PACK, spoilt, s)
    moved = exact(as_bf16((sub == hit_rank) & hit), spare1[...].reshape(ROWS, BLK))
    pack2[...] = jnp.where(sub == SPARE, second_keys, moved)
    for k, p in enumerate(scen_peers):
        second(k, p, s).start()
    pltpu.make_async_copy(pack2, spare2.at[s], second_recv.at[s]).start()

    cell = lax.broadcasted_iota(I32, (CLUS * OWN, ROWS), 0)
    for step in range(2):
        group = (z // 4 + step) % 2 * 8
        for a in range(8):
            message(0, s, group + a).wait_recv()
        key = landed[group, pl.ds(CAP, 1), :]
        for a in range(1, 8):
            key = key + landed[group + a, pl.ds(CAP, 1), :]
        part = exact(as_bf16(cell == key.astype(I32) - 1), landed[pl.ds(group, 8)].reshape(8 * MSG, BLK))
        total[...] = part if step == 0 else total[...] + part

    def row(k, e, src):
        return pltpu.make_async_remote_copy(
            src_ref=total.at[pl.ds(e * OWN, OWN), :], dst_ref=rows.at[src],
            send_sem=row_send.at[k], recv_sem=row_recv.at[src],
            device_id=(s, e), device_id_type=MESH,
        )

    for k, p in enumerate(clus_peers):
        row(k, p, i).start()
    pltpu.make_async_copy(total.at[pl.ds(i * OWN, OWN), :], rows.at[i], row_recv.at[i]).start()
    inverse.wait()
    for src in range(SCEN):
        second(0, s, src).wait_recv()
    valid, device, place, spoilt = read_keys(spare2)
    here = as_bf16(cell == jnp.where(valid & (device == s), place, -1))
    late[...] = exact(here, spare2[...].reshape(ROWS, BLK)).reshape(CLUS, OWN, BLK)
    flag[0, 0] = jnp.max(jnp.where(spoilt, 1, 0))
    for src in range(CLUS):
        row(0, i, src).wait_recv()
    for r in range(KC):
        line = rows[inv_s[r, 0]] + late[inv_s[r, 0]]
        for cb in range(OWN):
            out[pl.ds(r, 1), pl.ds(cb * BLK, BLK)] = line[cb : cb + 1]
    for k in range(15):
        message(k, scen_peers[k], s).wait_send()
        second(k, scen_peers[k], s).wait_send()
        first(k, clus_peers[k], i).wait_send()
        row(k, clus_peers[k], i).wait_send()


def body(duals, blocks, prob, cluster_map, block_cols, counts, cut_owner_rows):
    dma = pltpu.SemaphoreType.DMA
    arrays = (
        duals.reshape(ROWS, BLK),
        blocks.reshape(ROWS, BLK, BLK),
        prob.reshape(1, 64),
        cluster_map.reshape(1, 64),
        block_cols.T,
        counts.reshape(1, 1),
        cut_owner_rows,
        cut_owner_rows.reshape(1, 256),
    )
    inputs = [
        pltpu.VMEM((ROWS, BLK, BLK), BF16),
        pltpu.VMEM((ROWS, BLK), BF16),
        pltpu.VMEM((1, 64), F32),
        pltpu.VMEM((1, 64), I32),
        pltpu.VMEM((2, 64), I32),
        pltpu.SMEM((1, 1), I32),
        pltpu.SMEM((256,), I32),
        pltpu.VMEM((1, 256), I32),
        pltpu.VMEM((16, 128), I32),
        pltpu.SMEM((16, 128), I32),
    ]
    block = pltpu.VMEM((KC, OWN * BLK), F32)
    vmem = pl.BlockSpec(memory_space=pltpu.VMEM)

    def call(fn, shapes, specs, scratch, cid):
        return pl.pallas_call(
            fn,
            out_shape=shapes,
            in_specs=[pl.BlockSpec(memory_space=pltpu.HBM)] * len(arrays),
            out_specs=specs,
            scratch_shapes=inputs + scratch,
            compiler_params=pltpu.CompilerParams(
                collective_id=cid, has_side_effects=True, vmem_limit_bytes=60 << 20
            ),
        )(*arrays)

    def gathered():
        scratch = [
            pltpu.VMEM((SCEN, PIECE, BLK), F32),
            pltpu.VMEM((CLUS * OWN, BLK), F32),
            pltpu.VMEM((CLUS, OWN, BLK), F32),
            dma((8,)),
            dma((4,)),
            dma((2, 4, 4)),
            dma((2, 4, 4)),
            dma((2, 5, 4)),
            dma((2, 5, 4)),
            dma((CLUS,)),
            dma((CLUS,)),
        ]
        return call(kernel, block, vmem, scratch, 0)

    scratch = [
        pltpu.VMEM((ROWS, BLK), F32),
        pltpu.VMEM((SCEN, MSG, BLK), F32),
        pltpu.VMEM((SCEN, MSG, BLK), F32),
        pltpu.VMEM((CLUS * OWN, BLK), F32),
        pltpu.VMEM((CLUS, OWN, BLK), F32),
        pltpu.VMEM((PACK, BLK), F32),
        pltpu.VMEM((PACK, BLK), F32),
        pltpu.VMEM((CLUS, PACK, BLK), F32),
        pltpu.VMEM((SCEN, PACK, BLK), F32),
        pltpu.VMEM((CLUS, OWN, BLK), F32),
        dma((8,)),
        dma((4,)),
    ] + [dma((16,))] * 8
    flag = pltpu.SMEM((1, 1), I32)
    out, full = call(routed, (block, flag), (vmem, pl.BlockSpec(memory_space=pltpu.SMEM)), scratch, 1)
    return lax.switch(full[0, 0], (lambda: out, gathered))


def solution(mesh):
    placed = (
        P(("scen", "clus"), None, None),
        P(("scen", "clus"), None, None, None),
        P(("scen", "clus")),
        P(("scen", "clus")),
        P(("scen", "clus"), None),
        P(("scen", "clus")),
        P(),
    )
    return jax.shard_map(
        body, mesh=mesh, in_specs=placed, out_specs=P("clus", "scen"), check_vma=False
    )
```
